32 devices in a mesh: wide: 4 (over z), narrow: 8 (over y, x, core).
Axes of the slice: x: 2, y: 2, z: 4, core: 2. Of those that a mesh axis runs over, the one named last changes fastest.
Arguments:
- samples: bfloat16 [1024, 2, 102144], P(('wide', 'narrow')), may hold values from -6 to 6
- filter_taps: float32 [16, 256], replicated, may hold values from -1.5 to 1.5
- beam_weights: bfloat16 [256, 2, 2, 512, 1024], P(('narrow', 'wide')), may hold values from -0.1875 to 0.1875
- smooth_kernel: float32 [33, 33], replicated, may hold values from -0.1875 to 0.1875
Outputs:
- detection: float32 [256, 48, 1024], P('narrow', None, 'wide')
The draws below stay inside these ranges and needn't reach their ends.
All inputs are finite; a program needn't handle non-finite values.
Results may differ from the reference program's by a relative error of at most 0.012.
The reference program's roundings to bfloat16 on the way count: a program that leaves them out, or rounds other values in their place, can miss the bound.
Values may be sent and summed in bfloat16 or wider, within the bound.
A program may use at most 320 MiB of HBM per device.

```python
import jax
import jax.numpy as jnp
from jax import lax

DISHES = 512
POLS = 2
NFFT = 256
TAPS = 16
BEAMS = 1024
INTEG = 8
HALF = 16
SPECTRA = 384
INPUTS = 1024
CHANNELS = 256
TBINS = 48
SAMPLES = 102144


def levels(stream_key, dims, split, smallest, high):
    def one(axis_at, blocks):
        steps = jax.random.uniform(jax.random.fold_in(jax.random.fold_in(stream_key, 6), axis_at), (blocks,), jnp.float32, smallest / len(split), high / len(split))
        return jnp.repeat(jnp.exp(steps), dims[axis_at] // blocks).reshape((-1,) + (1,) * (len(dims) - axis_at - 1))

    gain = one(*split[0])
    for cut in split[1:]:
        gain = gain * one(*cut)
    return gain


def bell_draw(stream_key, shape, spread, reach, shards=(), kind=jnp.bfloat16):
    array = jax.random.normal(stream_key, shape, jnp.float32) * spread
    if len(shards) > 0:
        array = levels(stream_key, shape, shards, -0.22, 0.18) * array
    return jnp.clip(array, min=-reach, max=reach).astype(kind)


def setup_inputs(seed: int = 0) -> dict:
    arg_keys = jax.random.split(jax.random.key(seed), 5)
    return {
        "samples": bell_draw(arg_keys[0], (INPUTS, 2, SAMPLES), 1.0, 6.0, ((0, 32),)),
        "filter_taps": bell_draw(arg_keys[1], (TAPS, NFFT), TAPS ** -0.5, 1.5, (), jnp.float32),
        "beam_weights": bell_draw(arg_keys[2], (CHANNELS, POLS, 2, DISHES, BEAMS), (2 * DISHES) ** -0.5, 0.1875, ((0, 32),)),
        "smooth_kernel": bell_draw(arg_keys[3], (2 * HALF + 1, 2 * HALF + 1), ((2 * HALF + 1) * (2 * HALF + 1)) ** -0.5, 0.1875, (), jnp.float32),
    }


def fourier_rows(points):
    column = jnp.arange(points, dtype=jnp.int32)
    phase_index = (column[:, None] * column[None, :]) % points
    angles = phase_index.astype(jnp.float32) * jnp.float32(2.0 * jnp.pi / points)
    scale = jnp.float32(1.0 / (points ** 0.5))
    cosine = jnp.cos(angles) * scale
    sine_part = jnp.sin(angles) * scale
    real_row = jnp.stack([cosine, sine_part], axis=1)
    imag_row = jnp.stack([-sine_part, cosine], axis=1)
    return jnp.stack([real_row, imag_row], axis=1).reshape(2 * points, 2, points)


def channelize_one(signal_in, filter_taps, fourier_table):
    tap_count, points = filter_taps.shape
    frames = signal_in.shape[1] // points
    spectra = frames - tap_count + 1
    signal = signal_in.astype(jnp.float32).reshape(2, frames, points)
    windowed = filter_taps[0] * signal[:, 0:spectra]
    for tap_index in range(1, tap_count):
        windowed = windowed + filter_taps[tap_index] * signal[:, tap_index:tap_index + spectra]
    spectrum = jnp.einsum("pab,asb->ps", fourier_table, windowed, precision=lax.Precision.HIGH)
    return spectrum.astype(jnp.bfloat16).reshape(points, 2, spectra)


def channel_power(voltage, weights):
    values = voltage.astype(jnp.float32).reshape(POLS, DISHES, 2, SPECTRA)
    coeffs = weights.astype(jnp.float32)
    real_in = values[:, :, 0]
    imag_in = values[:, :, 1]
    real_w = coeffs[:, 0]
    imag_w = coeffs[:, 1]
    real_out = jnp.einsum("pds,pdb->psb", real_in, real_w) - jnp.einsum("pds,pdb->psb", imag_in, imag_w)
    imag_out = jnp.einsum("pds,pdb->psb", real_in, imag_w) + jnp.einsum("pds,pdb->psb", imag_in, real_w)
    energy = jnp.sum(real_out * real_out + imag_out * imag_out, axis=0)
    binned = energy.reshape(TBINS, INTEG, BEAMS).sum(axis=1)
    return (binned / jnp.float32(POLS * INTEG)).astype(jnp.bfloat16)


def reference(samples, filter_taps, beam_weights, smooth_kernel):
    fourier_table = fourier_rows(NFFT)

    def channelize_input(signal_in):
        return channelize_one(signal_in, filter_taps, fourier_table)

    voltage = lax.map(channelize_input, samples)
    by_channel = jnp.transpose(voltage, (1, 0, 2, 3))

    def power_of(paired):
        return channel_power(paired[0], paired[1])

    intensity = lax.map(power_of, (by_channel, beam_weights))
    values = intensity.astype(jnp.float32)
    centered = values - jnp.mean(values, axis=1, keepdims=True)
    image = jnp.transpose(centered, (2, 0, 1))[:, None]
    kernel = smooth_kernel[None, None]
    filtered = lax.conv_general_dilated(image, kernel, (1, 1), [(HALF, HALF), (HALF, HALF)], precision=lax.Precision.HIGH)
    return jnp.transpose(filtered[:, 0], (1, 2, 0))
```

```python
import dataclasses
import functools

import jax
import jax.numpy as jnp
from jax import lax
from jax.experimental import pallas as pl
from jax.experimental.pallas import tpu as pltpu
from jax.sharding import PartitionSpec as P

INTEG = 8
LANES = 128
BAND = 8
SLOTS = 3
LAG = 2
MESH = pl.DeviceIdType.MESH


@dataclasses.dataclass(frozen=True)
class Plan:
    wide: int
    narrow: int
    inputs: int
    per_device: int
    points: int
    taps: int
    pols: int
    dishes: int
    beams: int
    spectra: int

    @property
    def devices(self):
        return self.wide * self.narrow

    @property
    def groups(self):
        return max(1, self.inputs // 16)

    @property
    def rows(self):
        return self.inputs // self.groups

    @property
    def span(self):
        return LANES // (2 * self.groups)

    @property
    def chunks(self):
        return self.spectra // self.span

    @property
    def bins(self):
        return self.span // INTEG

    @property
    def halves(self):
        return self.points // LANES

    @property
    def tiles(self):
        return (self.span + self.taps - 1) * self.halves

    @property
    def per_pol(self):
        return self.devices // self.pols


def with_halo(block, sides, width):
    for axis, dim in sides:
        count = lax.axis_size(axis)
        forward = [(i, i + 1) for i in range(count - 1)]
        backward = [(target, source) for source, target in forward]
        low = lax.ppermute(
            lax.slice_in_dim(block, block.shape[dim] - width, None, axis=dim), axis, forward
        )
        high = lax.ppermute(lax.slice_in_dim(block, 0, width, axis=dim), axis, backward)
        block = jnp.concatenate([low, block, high], axis=dim)
    return block


def fourier_rows(points, owner_of):
    column = jnp.arange(points, dtype=jnp.int32)
    channel = owner_of(column)
    phase_index = channel[:, None] * column[None, :] % points
    angles = phase_index.astype(jnp.float32) * jnp.float32(2.0 * jnp.pi / points)
    scale = jnp.float32(1.0 / points**0.5)
    cosine = jnp.cos(angles) * scale
    sine_part = jnp.sin(angles) * scale
    real_row = jnp.concatenate([cosine, sine_part], axis=1)
    imag_row = jnp.concatenate([-sine_part, cosine], axis=1)
    return jnp.concatenate([real_row, imag_row], axis=0)


def split(value):
    high = value.astype(jnp.bfloat16)
    return high, (value - high.astype(jnp.float32)).astype(jnp.bfloat16)


def fused_kernel(
    plan,
    taps_ref,
    table_ref,
    samples_ref,
    weights_ref,
    recv_ref,
    intensity_ref,
    high_ref,
    low_ref,
    raw_ref,
    window_ref,
    stage_ref,
    send_ref,
    weight_ref,
    land_ref,
    energy_ref,
    raw_sem,
    weight_sem,
    send_sem,
    recv_sem,
    land_sem,
):
    span, rows, groups, halves = plan.span, plan.rows, plan.groups, plan.halves
    tap_count, points, chunks = plan.taps, plan.points, plan.chunks
    my_wide = lax.axis_index("wide")
    my_narrow = lax.axis_index("narrow")
    me = my_wide * plan.narrow + my_narrow

    def peer(step):
        return (
            lax.rem(my_wide + step // plan.narrow, plan.wide),
            lax.rem(my_narrow + step % plan.narrow, plan.narrow),
        )

    def load_raw(chunk, slot):
        @pl.loop(0, plan.tiles)
        def _(tile):
            column = pl.multiple_of((chunk * span * halves + tile) * LANES, LANES)
            pltpu.make_async_copy(
                samples_ref.at[:, :, pl.ds(column, LANES)], raw_ref.at[slot, tile], raw_sem.at[slot]
            ).start()

    barrier = pltpu.get_barrier_semaphore()
    load_raw(0, 0)

    @pl.loop(1, plan.devices)
    def _(step):
        pl.semaphore_signal(barrier, inc=1, device_id=peer(step), device_id_type=MESH)

    @pl.loop(0, plan.per_device)
    def _(channel):
        pltpu.make_async_copy(
            weights_ref.at[channel], weight_ref.at[channel], weight_sem
        ).start()

    high_ref[...], low_ref[...] = split(table_ref[...])

    def filter_rows(slot):
        row_groups = 2 * plan.inputs // 8

        @pl.loop(0, halves * row_groups)
        def _(index):
            half = index // row_groups
            group = index % row_groups
            coeffs = [
                jnp.broadcast_to(taps_ref[half, tap : tap + 1, :], (8, LANES))
                for tap in range(tap_count)
            ]
            sums = {}
            for frame in range(span + tap_count - 1):
                piece = raw_ref[slot, frame * halves + half, pl.ds(group * 4, 4)]
                value = piece.reshape(8, LANES).astype(jnp.float32)
                for out in range(max(0, frame - tap_count + 1), min(span - 1, frame) + 1):
                    term = coeffs[frame - out] * value
                    sums[out] = sums[out] + term if out in sums else term
                done = frame - tap_count + 1
                if done >= 0:
                    base = group * (8 * span) + done
                    window_ref[half, pl.ds(base, 8, stride=span), :] = sums.pop(done)

    def transform(slot):
        lane = lax.broadcasted_iota(jnp.int32, (points, LANES), 1)
        first = lane % (2 * span) < span
        product = functools.partial(
            lax.dot_general,
            dimension_numbers=(((1,), (1,)), ((), ())),
            preferred_element_type=jnp.float32,
        )
        pairs = 2

        @pl.loop(0, rows // (2 * pairs))
        def _(step):
            pieces = []
            for pair in range(pairs):
                for group in range(groups):
                    for member in range(2):
                        source = group * rows + step * (2 * pairs) + 2 * pair + member
                        blocks = []
                        for part in range(2):
                            start = pl.multiple_of((2 * source + part) * span, span)
                            for half in range(halves):
                                blocks.append(window_ref[half, pl.ds(start, span), :])
                        pieces.append(jnp.concatenate(blocks, axis=1))
            high, low = split(jnp.concatenate(pieces, axis=0))
            result = (
                product(low_ref[...], high)
                + product(high_ref[...], low)
                + product(high_ref[...], high)
            )
            for pair in range(pairs):
                real = result[:points, pair * LANES : (pair + 1) * LANES]
                imag = result[points:, pair * LANES : (pair + 1) * LANES]
                row = step * (2 * pairs) + 2 * pair
                stage_ref[pl.ds(row, points, stride=rows), :] = jnp.where(
                    first, real, pltpu.roll(imag, span, 1)
                )
                stage_ref[pl.ds(row + 1, points, stride=rows), :] = jnp.where(
                    first, pltpu.roll(real, LANES - span, 1), imag
                )

        send_ref[slot] = stage_ref[...].reshape(points, rows, LANES).astype(jnp.bfloat16)

    def start_sends(chunk, slot):
        @pl.loop(1, plan.devices)
        def _(step):
            wide, narrow = peer(step)
            target = wide * plan.narrow + narrow
            pltpu.make_async_remote_copy(
                src_ref=send_ref.at[slot, pl.ds(target * plan.per_device, plan.per_device)],
                dst_ref=recv_ref.at[chunk, me],
                send_sem=send_sem.at[slot],
                recv_sem=recv_sem.at[chunk],
                device_id=(wide, narrow),
                device_id_type=MESH,
            ).start()

        pltpu.make_async_copy(
            send_ref.at[slot, pl.ds(me * plan.per_device, plan.per_device)],
            recv_ref.at[chunk, me],
            recv_sem.at[chunk],
        ).start()

    def wait_sends(slot):
        sent = send_ref.at[slot, pl.ds(0, (plan.devices - 1) * plan.per_device)]
        pltpu.make_async_copy(sent, sent, send_sem.at[slot]).wait()

    def form_beams(chunk):
        arrived = recv_ref.at[chunk]
        pltpu.make_async_copy(arrived, arrived, recv_sem.at[chunk]).wait()
        landing = pltpu.make_async_copy(arrived, land_ref, land_sem)
        landing.start()
        landing.wait()
        together = 8 // plan.bins

        @pl.loop(0, plan.per_device // together)
        def _(step):
            binned = []
            for member in range(together):
                channel = step * together + member
                energy = None
                for pol in range(plan.pols):
                    block = land_ref[pol * plan.per_pol : (pol + 1) * plan.per_pol, channel]
                    block = block.astype(jnp.float32).reshape(plan.per_pol * rows, LANES)
                    turned = block.T.astype(jnp.bfloat16)
                    formed = None
                    for group in range(groups):
                        base = 2 * span * group
                        straight = turned[base : base + 2 * span]
                        crossed = jnp.concatenate(
                            [-straight[span:], straight[:span]], axis=0
                        )
                        for side, left in enumerate((straight, crossed)):
                            right = weight_ref[channel, pol, side, :, group]
                            right = right.reshape(-1, plan.beams)
                            term = jnp.dot(left, right, preferred_element_type=jnp.float32)
                            formed = term if formed is None else formed + term
                    squares = formed * formed
                    power = squares[:span] + squares[span:]
                    energy = power if energy is None else energy + power
                binned.append(energy.reshape(plan.bins, INTEG, plan.beams).sum(axis=1))
            energy_ref[pl.ds(pl.multiple_of(step * 8, 8), 8), :] = jnp.concatenate(
                binned, axis=0
            )

        scale = jnp.float32(1.0 / (plan.pols * INTEG))
        intensity_ref[chunk] = (energy_ref[...] * scale).astype(jnp.bfloat16)

    @pl.loop(0, chunks + LAG)
    def _(step):
        @pl.when(step < chunks)
        def _():
            side = step % 2
            slot = step % SLOTS
            raw = raw_ref.at[side]
            pltpu.make_async_copy(raw, raw, raw_sem.at[side]).wait()

            @pl.when(step + 1 < chunks)
            def _():
                load_raw(step + 1, 1 - side)

            filter_rows(side)

            @pl.when(step >= SLOTS)
            def _():
                wait_sends(slot)

            transform(slot)

            @pl.when(step == 0)
            def _():
                pl.semaphore_wait(barrier, plan.devices - 1)

            start_sends(step, slot)

        @pl.when(step == LAG)
        def _():
            pltpu.make_async_copy(weight_ref, weight_ref, weight_sem).wait()

        @pl.when(step >= LAG)
        def _():
            form_beams(step - LAG)

    for slot in range(min(SLOTS, chunks)):
        wait_sends(slot)


def fused(samples, filter_taps, table, beam_weights, plan):
    taps = filter_taps.reshape(plan.taps, plan.halves, LANES).transpose(1, 0, 2)
    if plan.groups == 1:
        dish_split = (1, 1, plan.dishes)
    else:
        dish_split = (plan.per_pol, plan.groups, plan.rows)
    weight_shape = (plan.per_device, plan.pols, 2, *dish_split, plan.beams)
    weights = beam_weights.reshape(weight_shape)
    anywhere = pl.BlockSpec(memory_space=pl.ANY)
    local = pl.BlockSpec(memory_space=pltpu.VMEM)
    recv_shape = (plan.chunks, plan.devices, plan.per_device, plan.rows, LANES)
    energy_shape = (plan.per_device * plan.bins, plan.beams)
    return pl.pallas_call(
        functools.partial(fused_kernel, plan),
        in_specs=[local, local, anywhere, anywhere],
        out_specs=[anywhere, local],
        out_shape=[
            jax.ShapeDtypeStruct(recv_shape, jnp.bfloat16),
            jax.ShapeDtypeStruct((plan.chunks, *energy_shape), jnp.bfloat16),
        ],
        scratch_shapes=[
            pltpu.VMEM(table.shape, jnp.bfloat16),
            pltpu.VMEM(table.shape, jnp.bfloat16),
            pltpu.VMEM((2, plan.tiles, plan.inputs, 2, LANES), jnp.bfloat16),
            pltpu.VMEM((plan.halves, 2 * plan.inputs * plan.span, LANES), jnp.float32),
            pltpu.VMEM((plan.points * plan.rows, LANES), jnp.float32),
            pltpu.VMEM((SLOTS, plan.points, plan.rows, LANES), jnp.bfloat16),
            pltpu.VMEM(weight_shape, jnp.bfloat16),
            pltpu.VMEM(recv_shape[1:], jnp.bfloat16),
            pltpu.VMEM(energy_shape, jnp.float32),
            pltpu.SemaphoreType.DMA((2,)),
            pltpu.SemaphoreType.DMA,
            pltpu.SemaphoreType.DMA((SLOTS,)),
            pltpu.SemaphoreType.DMA((plan.chunks,)),
            pltpu.SemaphoreType.DMA,
        ],
        compiler_params=pltpu.CompilerParams(
            collective_id=0, has_side_effects=True, vmem_limit_bytes=66 * 1000 * 1000
        ),
        name="fused",
    )(taps, table, samples, weights)[1]


def band_matrix(smooth_kernel, bin_count):
    extent = smooth_kernel.shape[0]
    half_width = extent // 2
    span = BAND + extent - 1
    offsets = jnp.arange(extent, dtype=jnp.int32)
    bins = jnp.arange(bin_count, dtype=jnp.int32)
    distance = bins[None, :] - bins[:, None] + half_width
    in_time = (distance[None] == offsets[:, None, None]).astype(jnp.float32)
    steps = jnp.arange(span, dtype=jnp.int32)[None, :] - jnp.arange(BAND, dtype=jnp.int32)[:, None]
    in_band = (steps[None] == offsets[:, None, None]).astype(jnp.float32)
    rows = jnp.einsum("kcj,kd->cjd", in_band, smooth_kernel, precision=lax.Precision.HIGHEST)
    matrix = jnp.einsum("cjd,dtu->ctju", rows, in_time, precision=lax.Precision.HIGHEST)
    return matrix.reshape(BAND * bin_count, span * bin_count)


def smooth(extended, matrix, half_width):
    channels_here = extended.shape[0] - 2 * half_width
    bin_count, beams = extended.shape[1:]
    values = extended.astype(jnp.float32)
    centered = values - jnp.mean(values, axis=1, keepdims=True)
    flat = centered.reshape(-1, beams)
    pieces = []
    for start in range(0, channels_here, BAND):
        rows = lax.slice_in_dim(flat, start * bin_count, start * bin_count + matrix.shape[1], axis=0)
        pieces.append(
            jnp.dot(
                matrix, rows, precision=lax.Precision.HIGH, preferred_element_type=jnp.float32
            )
        )
    return jnp.concatenate(pieces, axis=0).reshape(channels_here, bin_count, beams)


def body(samples, filter_taps, beam_weights, smooth_kernel):
    tap_count, points = filter_taps.shape
    wide_count = lax.axis_size("wide")
    narrow_count = lax.axis_size("narrow")
    per_device, pols, _, dishes, beams = beam_weights.shape
    frames = samples.shape[2] // points
    plan = Plan(
        wide=wide_count,
        narrow=narrow_count,
        inputs=samples.shape[0],
        per_device=per_device,
        points=points,
        taps=tap_count,
        pols=pols,
        dishes=dishes,
        beams=beams,
        spectra=frames - tap_count + 1,
    )

    def owner_of(column):
        device_slot = column // per_device
        return (
            device_slot % narrow_count * wide_count + device_slot // narrow_count
        ) * per_device + column % per_device

    table = fourier_rows(points, owner_of)
    matrix = band_matrix(smooth_kernel, plan.spectra // INTEG)
    pieces = fused(samples, filter_taps, table, beam_weights, plan)
    intensity = pieces.reshape(plan.chunks, per_device, plan.bins, wide_count, beams // wide_count)
    intensity = intensity.transpose(3, 1, 0, 2, 4)
    intensity = intensity.reshape(wide_count, per_device, -1, beams // wide_count)
    by_beam = lax.all_to_all(intensity, "wide", split_axis=0, concat_axis=0, tiled=True)
    by_beam = by_beam.reshape(-1, *by_beam.shape[2:])
    half_width = smooth_kernel.shape[0] // 2
    extended = with_halo(by_beam, (("narrow", 0),), half_width)
    return smooth(extended, matrix, half_width)


def solution(mesh):
    placed = (
        P(("wide", "narrow"), None, None),
        P(),
        P(("narrow", "wide"), None, None, None, None),
        P(),
    )
    return jax.shard_map(
        body, mesh=mesh, in_specs=placed, out_specs=P("narrow", None, "wide"), check_vma=False
    )
```

```python
import dataclasses
import functools

import jax
import jax.numpy as jnp
import numpy as np
from jax import lax
from jax.experimental import pallas as pl
from jax.experimental.pallas import tpu as pltpu
from jax.sharding import PartitionSpec as P

INTEG = 8
LANES = 128
BAND = 8
SLOTS = 3
LAG = 2
HALO_LAG = 4
SMOOTH_LAG = 5
MESH = pl.DeviceIdType.MESH


@dataclasses.dataclass(frozen=True)
class Plan:
    wide: int
    narrow: int
    inputs: int
    per_device: int
    points: int
    taps: int
    pols: int
    dishes: int
    beams: int
    spectra: int
    extent: int

    @property
    def devices(self):
        return self.wide * self.narrow

    @property
    def groups(self):
        return max(1, self.inputs // 16)

    @property
    def rows(self):
        return self.inputs // self.groups

    @property
    def span(self):
        return LANES // (2 * self.groups)

    @property
    def chunks(self):
        return self.spectra // self.span

    @property
    def bins(self):
        return self.span // INTEG

    @property
    def halves(self):
        return self.points // LANES

    @property
    def tiles(self):
        return (self.span + self.taps - 1) * self.halves

    @property
    def per_pol(self):
        return self.devices // self.pols

    @property
    def half(self):
        return self.extent // 2

    @property
    def share(self):
        return self.beams // self.wide

    @property
    def local(self):
        return self.wide * self.per_device

    @property
    def all_bins(self):
        return self.spectra // INTEG

    @property
    def reach(self):
        return (BAND + self.extent - 1) * self.bins

    @property
    def lanes(self):
        return -(-self.reach // LANES) * LANES

    @property
    def shifts(self):
        return -(-(2 * self.all_bins - self.bins) // 8) * 8


def fourier_rows(points, owner_of):
    column = np.arange(points)
    phase_index = owner_of(column)[:, None] * column[None, :] % points
    angles = phase_index * (2.0 * np.pi / points)
    cosine = np.cos(angles) / np.sqrt(points)
    sine_part = np.sin(angles) / np.sqrt(points)
    real_row = np.concatenate([cosine, sine_part], axis=1)
    imag_row = np.concatenate([-sine_part, cosine], axis=1)
    table = np.concatenate([real_row, imag_row], axis=0).astype(np.float32)
    high = table.astype(jnp.bfloat16)
    return np.stack([high, (table - high.astype(np.float32)).astype(jnp.bfloat16)])


def one_hot(shape, matches):
    row = lax.broadcasted_iota(jnp.int32, shape, 0)
    column = lax.broadcasted_iota(jnp.int32, shape, 1)
    return matches(row, column).astype(jnp.float32)


def exact_dot(left, right, contract=(1, 0)):
    return lax.dot_general(
        left,
        right,
        (((contract[0],), (contract[1],)), ((), ())),
        precision=lax.Precision.HIGHEST,
        preferred_element_type=jnp.float32,
    )


def split(value):
    high = value.astype(jnp.bfloat16)
    return high, (value - high.astype(jnp.float32)).astype(jnp.bfloat16)


def fused_kernel(
    plan,
    taps_ref,
    smooth_ref,
    table_hbm,
    samples_ref,
    weights_ref,
    recv_ref,
    out_ref,
    table_ref,
    raw_ref,
    window_ref,
    stage_ref,
    send_ref,
    weight_ref,
    land_ref,
    energy_ref,
    shifted_ref,
    matrix_ref,
    outgoing_ref,
    gather_ref,
    raw_sem,
    table_sem,
    weight_sem,
    send_sem,
    recv_sem,
    land_sem,
    share_sem,
    gather_sem,
    up_sem,
    down_sem,
    low_sem,
    high_sem,
):
    span, rows, groups, halves = plan.span, plan.rows, plan.groups, plan.halves
    tap_count, points, chunks = plan.taps, plan.points, plan.chunks
    my_wide = lax.axis_index("wide")
    my_narrow = lax.axis_index("narrow")
    me = my_wide * plan.narrow + my_narrow

    def peer(step):
        return (
            lax.rem(my_wide + step // plan.narrow, plan.wide),
            lax.rem(my_narrow + step % plan.narrow, plan.narrow),
        )

    def load_raw(chunk, slot):
        @pl.loop(0, plan.tiles)
        def _(tile):
            column = pl.multiple_of((chunk * span * halves + tile) * LANES, LANES)
            pltpu.make_async_copy(
                samples_ref.at[:, :, pl.ds(column, LANES)], raw_ref.at[slot, tile], raw_sem.at[slot]
            ).start()

    own_start = plan.half * plan.bins
    own_rows = plan.local * plan.bins
    part_rows = plan.per_device * plan.bins

    barrier = pltpu.get_barrier_semaphore()
    load_raw(0, 0)
    pltpu.make_async_copy(table_hbm, table_ref, table_sem).start()

    @pl.loop(1, plan.devices)
    def _(step):
        pl.semaphore_signal(barrier, inc=1, device_id=peer(step), device_id_type=MESH)

    @pl.loop(0, plan.per_device)
    def _(channel):
        pltpu.make_async_copy(
            weights_ref.at[channel], weight_ref.at[channel], weight_sem
        ).start()

    out_ref[...] = jnp.zeros_like(out_ref)

    def clear(start):
        gather_ref[:, start : start + own_start] = jnp.zeros(
            (chunks, own_start, plan.share), jnp.bfloat16
        )

    @pl.when(my_narrow == 0)
    def _():
        clear(0)

    @pl.when(my_narrow == plan.narrow - 1)
    def _():
        clear(own_start + own_rows)

    def filter_rows(slot):
        row_groups = 2 * plan.inputs // 8

        @pl.loop(0, halves * row_groups)
        def _(index):
            half = index // row_groups
            group = index % row_groups
            columns = pl.ds(pl.multiple_of(half * LANES, LANES), LANES)
            coeffs = [
                jnp.broadcast_to(taps_ref[tap : tap + 1, columns], (8, LANES))
                for tap in range(tap_count)
            ]
            sums = {}
            for frame in range(span + tap_count - 1):
                piece = raw_ref[slot, frame * halves + half, pl.ds(group * 4, 4)]
                value = piece.reshape(8, LANES).astype(jnp.float32)
                for out in range(max(0, frame - tap_count + 1), min(span - 1, frame) + 1):
                    term = coeffs[frame - out] * value
                    sums[out] = sums[out] + term if out in sums else term
                done = frame - tap_count + 1
                if done >= 0:
                    base = group * (8 * span) + done
                    window_ref[half, pl.ds(base, 8, stride=span), :] = sums.pop(done)

    def transform(slot):
        lane = lax.broadcasted_iota(jnp.int32, (points, LANES), 1)
        first = lane % (2 * span) < span
        product = functools.partial(
            lax.dot_general,
            dimension_numbers=(((1,), (1,)), ((), ())),
            preferred_element_type=jnp.float32,
        )
        pairs = 2

        @pl.loop(0, rows // (2 * pairs))
        def _(step):
            pieces = []
            for pair in range(pairs):
                for group in range(groups):
                    for member in range(2):
                        source = group * rows + step * (2 * pairs) + 2 * pair + member
                        blocks = []
                        for part in range(2):
                            start = pl.multiple_of((2 * source + part) * span, span)
                            for half in range(halves):
                                blocks.append(window_ref[half, pl.ds(start, span), :])
                        pieces.append(jnp.concatenate(blocks, axis=1))
            high, low = split(jnp.concatenate(pieces, axis=0))
            result = (
                product(table_ref[1], high)
                + product(table_ref[0], low)
                + product(table_ref[0], high)
            )
            for pair in range(pairs):
                real = result[:points, pair * LANES : (pair + 1) * LANES]
                imag = result[points:, pair * LANES : (pair + 1) * LANES]
                row = step * (2 * pairs) + 2 * pair
                stage_ref[pl.ds(row, points, stride=rows), :] = jnp.where(
                    first, real, pltpu.roll(imag, span, 1)
                )
                stage_ref[pl.ds(row + 1, points, stride=rows), :] = jnp.where(
                    first, pltpu.roll(real, LANES - span, 1), imag
                )

        send_ref[slot] = stage_ref[...].reshape(points, rows, LANES).astype(jnp.bfloat16)

    def start_sends(chunk, slot):
        @pl.loop(1, plan.devices)
        def _(step):
            wide, narrow = peer(step)
            target = wide * plan.narrow + narrow
            pltpu.make_async_remote_copy(
                src_ref=send_ref.at[slot, pl.ds(target * plan.per_device, plan.per_device)],
                dst_ref=recv_ref.at[chunk, me],
                send_sem=send_sem.at[slot],
                recv_sem=recv_sem.at[chunk],
                device_id=(wide, narrow),
                device_id_type=MESH,
            ).start()

        pltpu.make_async_copy(
            send_ref.at[slot, pl.ds(me * plan.per_device, plan.per_device)],
            recv_ref.at[chunk, me],
            recv_sem.at[chunk],
        ).start()

    def wait_sends(slot):
        sent = send_ref.at[slot, pl.ds(0, (plan.devices - 1) * plan.per_device)]
        pltpu.make_async_copy(sent, sent, send_sem.at[slot]).wait()

    def form_beams(chunk):
        arrived = recv_ref.at[chunk]
        pltpu.make_async_copy(arrived, arrived, recv_sem.at[chunk]).wait()
        landing = pltpu.make_async_copy(arrived, land_ref, land_sem)
        landing.start()
        landing.wait()
        together = 8 // plan.bins

        @pl.loop(0, plan.per_device // together)
        def _(step):
            binned = []
            for member in range(together):
                channel = step * together + member
                energy = None
                for pol in range(plan.pols):
                    block = land_ref[pol * plan.per_pol : (pol + 1) * plan.per_pol, channel]
                    block = block.astype(jnp.float32).reshape(plan.per_pol * rows, LANES)
                    turned = block.T.astype(jnp.bfloat16)
                    formed = None
                    for group in range(groups):
                        base = 2 * span * group
                        straight = turned[base : base + 2 * span]
                        crossed = jnp.concatenate(
                            [-straight[span:], straight[:span]], axis=0
                        )
                        for side, left in enumerate((straight, crossed)):
                            right = weight_ref[channel, pol, side, :, group]
                            right = right.reshape(-1, plan.beams)
                            term = jnp.dot(left, right, preferred_element_type=jnp.float32)
                            formed = term if formed is None else formed + term
                    squares = formed * formed
                    power = squares[:span] + squares[span:]
                    energy = power if energy is None else energy + power
                binned.append(energy.reshape(plan.bins, INTEG, plan.beams).sum(axis=1))
            energy_ref[pl.ds(pl.multiple_of(step * 8, 8), 8), :] = jnp.concatenate(
                binned, axis=0
            )

        scale = jnp.float32(1.0 / (plan.pols * INTEG))
        intensity = (energy_ref[...] * scale).astype(jnp.bfloat16)
        for owner in range(plan.wide):
            outgoing_ref[chunk, owner] = intensity[:, owner * plan.share : (owner + 1) * plan.share]

        mine = pl.ds(pl.multiple_of(own_start + my_wide * part_rows, part_rows), part_rows)

        @pl.loop(1, plan.wide)
        def _(step):
            target = lax.rem(my_wide + step, plan.wide)
            pltpu.make_async_remote_copy(
                src_ref=outgoing_ref.at[chunk, target],
                dst_ref=gather_ref.at[chunk, mine],
                send_sem=share_sem.at[chunk],
                recv_sem=gather_sem.at[chunk],
                device_id=(target, my_narrow),
                device_id_type=MESH,
            ).start()

        pltpu.make_async_copy(
            outgoing_ref.at[chunk, my_wide], gather_ref.at[chunk, mine], gather_sem.at[chunk]
        ).start()

    def halo(chunk):
        def upward():
            return pltpu.make_async_remote_copy(
                src_ref=gather_ref.at[chunk, pl.ds(own_rows, own_start)],
                dst_ref=gather_ref.at[chunk, pl.ds(0, own_start)],
                send_sem=up_sem.at[chunk],
                recv_sem=low_sem.at[chunk],
                device_id=(my_wide, my_narrow + 1),
                device_id_type=MESH,
            )

        def downward():
            return pltpu.make_async_remote_copy(
                src_ref=gather_ref.at[chunk, pl.ds(own_start, own_start)],
                dst_ref=gather_ref.at[chunk, pl.ds(own_start + own_rows, own_start)],
                send_sem=down_sem.at[chunk],
                recv_sem=high_sem.at[chunk],
                device_id=(my_wide, my_narrow - 1),
                device_id_type=MESH,
            )

        return upward, downward

    def start_halo(chunk):
        own = gather_ref.at[chunk, pl.ds(own_start, own_rows)]
        pltpu.make_async_copy(own, own, gather_sem.at[chunk]).wait()
        upward, downward = halo(chunk)

        @pl.when(my_narrow < plan.narrow - 1)
        def _():
            upward().start()

        @pl.when(my_narrow > 0)
        def _():
            downward().start()

    def build_matrix():
        extent, bins, shifts, lanes = plan.extent, plan.bins, plan.shifts, plan.lanes
        last = plan.all_bins - bins
        spread = one_hot((extent, lanes), lambda row, column: row == column // bins)
        columns = exact_dot(smooth_ref[...], spread, (0, 0))
        inner = lax.broadcasted_iota(jnp.int32, (shifts, lanes), 1) % bins
        shifted = jnp.zeros((shifts, lanes), jnp.float32)
        for offset in range(bins):
            select = one_hot(
                (shifts, extent),
                lambda row, column: column == offset - row + last + plan.half,
            )
            shifted = jnp.where(inner == offset, exact_dot(select, columns), shifted)
        shifted_ref[...] = shifted
        gather = one_hot(
            (plan.all_bins, shifts),
            lambda row, column: (column >= row)
            & (column <= row + last)
            & ((column - row) % bins == 0),
        )
        block = one_hot((lanes, lanes), lambda row, column: row // bins == column // bins)
        total = exact_dot(exact_dot(gather, shifted), block)
        mean = total * jnp.float32(1.0 / plan.all_bins)

        @pl.loop(0, chunks)
        def _(chunk):
            start = shifts - (last - bins * chunk)
            rows_here = pltpu.roll(shifted_ref[...], lax.rem(start, shifts), 0)[: plan.all_bins]
            centered = rows_here - mean
            for channel in range(BAND):
                moved = pltpu.roll(centered, bins * channel, 1) if channel else centered
                place = slice(channel * plan.all_bins, (channel + 1) * plan.all_bins)
                matrix_ref[chunk, 0, place], matrix_ref[chunk, 1, place] = split(moved)

    def smooth(chunk):
        upward, downward = halo(chunk)

        @pl.when(my_narrow > 0)
        def _():
            upward().wait_recv()

        @pl.when(my_narrow < plan.narrow - 1)
        def _():
            downward().wait_recv()

        for band in range(plan.local // BAND):
            start = band * BAND * plan.bins
            values = gather_ref[chunk, start : start + plan.reach]
            size = BAND * plan.all_bins
            place = slice(band * size, (band + 1) * size)
            total = out_ref[place]
            for side in (1, 0):
                total = total + jnp.dot(
                    matrix_ref[chunk, side, :, : plan.reach],
                    values,
                    preferred_element_type=jnp.float32,
                )
            out_ref[place] = total

    @pl.loop(0, chunks + SMOOTH_LAG)
    def _(step):
        @pl.when(step < chunks)
        def _():
            side = step % 2
            slot = step % SLOTS
            raw = raw_ref.at[side]
            pltpu.make_async_copy(raw, raw, raw_sem.at[side]).wait()

            @pl.when(step + 1 < chunks)
            def _():
                load_raw(step + 1, 1 - side)

            filter_rows(side)

            @pl.when(step >= SLOTS)
            def _():
                wait_sends(slot)

            @pl.when(step == 0)
            def _():
                pltpu.make_async_copy(table_hbm, table_ref, table_sem).wait()

            transform(slot)

            @pl.when(step == 0)
            def _():
                pl.semaphore_wait(barrier, plan.devices - 1)

            start_sends(step, slot)

        @pl.when(step == LAG)
        def _():
            build_matrix()
            pltpu.make_async_copy(weight_ref, weight_ref, weight_sem).wait()

        @pl.when((step >= LAG) & (step < chunks + LAG))
        def _():
            form_beams(step - LAG)

        @pl.when((step >= HALO_LAG) & (step < chunks + HALO_LAG))
        def _():
            start_halo(step - HALO_LAG)

        @pl.when(step >= SMOOTH_LAG)
        def _():
            smooth(step - SMOOTH_LAG)

    for slot in range(min(SLOTS, chunks)):
        wait_sends(slot)

    @pl.loop(0, chunks)
    def _(chunk):
        sent = outgoing_ref.at[chunk, pl.ds(0, plan.wide - 1)]
        pltpu.make_async_copy(sent, sent, share_sem.at[chunk]).wait()
        upward, downward = halo(chunk)

        @pl.when(my_narrow < plan.narrow - 1)
        def _():
            upward().wait_send()

        @pl.when(my_narrow > 0)
        def _():
            downward().wait_send()


def fused(samples, filter_taps, table, beam_weights, smooth_kernel, plan):
    if plan.groups == 1:
        dish_split = (1, 1, plan.dishes)
    else:
        dish_split = (plan.per_pol, plan.groups, plan.rows)
    weight_shape = (plan.per_device, plan.pols, 2, *dish_split, plan.beams)
    weights = beam_weights.reshape(weight_shape)
    anywhere = pl.BlockSpec(memory_space=pl.ANY)
    local = pl.BlockSpec(memory_space=pltpu.VMEM)
    recv_shape = (plan.chunks, plan.devices, plan.per_device, plan.rows, LANES)
    energy_shape = (plan.per_device * plan.bins, plan.beams)
    ext_rows = (plan.local + 2 * plan.half) * plan.bins
    out_shape = (plan.local * plan.all_bins, plan.share)
    per_chunk = pltpu.SemaphoreType.DMA((plan.chunks,))
    return pl.pallas_call(
        functools.partial(fused_kernel, plan),
        in_specs=[local, local, anywhere, anywhere, anywhere],
        out_specs=[anywhere, local],
        out_shape=[
            jax.ShapeDtypeStruct(recv_shape, jnp.bfloat16),
            jax.ShapeDtypeStruct(out_shape, jnp.float32),
        ],
        scratch_shapes=[
            pltpu.VMEM(table.shape, jnp.bfloat16),
            pltpu.VMEM((2, plan.tiles, plan.inputs, 2, LANES), jnp.bfloat16),
            pltpu.VMEM((plan.halves, 2 * plan.inputs * plan.span, LANES), jnp.float32),
            pltpu.VMEM((plan.points * plan.rows, LANES), jnp.float32),
            pltpu.VMEM((SLOTS, plan.points, plan.rows, LANES), jnp.bfloat16),
            pltpu.VMEM(weight_shape, jnp.bfloat16),
            pltpu.VMEM(recv_shape[1:], jnp.bfloat16),
            pltpu.VMEM(energy_shape, jnp.float32),
            pltpu.VMEM((plan.shifts, plan.lanes), jnp.float32),
            pltpu.VMEM((plan.chunks, 2, BAND * plan.all_bins, plan.lanes), jnp.bfloat16),
            pltpu.VMEM(
                (plan.chunks, plan.wide, plan.per_device * plan.bins, plan.share), jnp.bfloat16
            ),
            pltpu.VMEM((plan.chunks, ext_rows, plan.share), jnp.bfloat16),
            pltpu.SemaphoreType.DMA((2,)),
            pltpu.SemaphoreType.DMA,
            pltpu.SemaphoreType.DMA,
            pltpu.SemaphoreType.DMA((SLOTS,)),
            per_chunk,
            pltpu.SemaphoreType.DMA,
            *([per_chunk] * 6),
        ],
        compiler_params=pltpu.CompilerParams(
            collective_id=0, has_side_effects=True, vmem_limit_bytes=66 * 1000 * 1000
        ),
        name="fused",
    )(filter_taps, smooth_kernel, table, samples, weights)[1]


def body(samples, filter_taps, beam_weights, smooth_kernel):
    tap_count, points = filter_taps.shape
    wide_count = lax.axis_size("wide")
    narrow_count = lax.axis_size("narrow")
    per_device, pols, _, dishes, beams = beam_weights.shape
    frames = samples.shape[2] // points
    plan = Plan(
        wide=wide_count,
        narrow=narrow_count,
        inputs=samples.shape[0],
        per_device=per_device,
        points=points,
        taps=tap_count,
        pols=pols,
        dishes=dishes,
        beams=beams,
        spectra=frames - tap_count + 1,
        extent=smooth_kernel.shape[0],
    )

    def owner_of(column):
        device_slot = column // per_device
        return (
            device_slot % narrow_count * wide_count + device_slot // narrow_count
        ) * per_device + column % per_device

    table = jnp.asarray(fourier_rows(points, owner_of))
    filtered = fused(samples, filter_taps, table, beam_weights, smooth_kernel, plan)
    return filtered.reshape(plan.local, plan.all_bins, plan.share)


def solution(mesh):
    placed = (
        P(("wide", "narrow"), None, None),
        P(),
        P(("narrow", "wide"), None, None, None, None),
        P(),
    )
    return jax.shard_map(
        body, mesh=mesh, in_specs=placed, out_specs=P("narrow", None, "wide"), check_vma=False
    )
```

```python
import dataclasses
import functools

import jax
import jax.numpy as jnp
import numpy as np
from jax import lax
from jax.experimental import pallas as pl
from jax.experimental.pallas import tpu as pltpu
from jax.sharding import PartitionSpec as P

INTEG = 8
LANES = 128
BAND = 8
SLOTS = 3
LAG = 2
HALO_LAG = 4
SMOOTH_LAG = 5
MESH = pl.DeviceIdType.MESH


@dataclasses.dataclass(frozen=True)
class Plan:
    wide: int
    narrow: int
    inputs: int
    per_device: int
    points: int
    taps: int
    pols: int
    dishes: int
    beams: int
    spectra: int
    extent: int

    @property
    def devices(self):
        return self.wide * self.narrow

    @property
    def groups(self):
        return max(1, self.inputs // 16)

    @property
    def rows(self):
        return self.inputs // self.groups

    @property
    def span(self):
        return LANES // (2 * self.groups)

    @property
    def chunks(self):
        return self.spectra // self.span

    @property
    def bins(self):
        return self.span // INTEG

    @property
    def together(self):
        return 8 // self.bins

    @property
    def sets(self):
        return self.per_device // self.together

    @property
    def halves(self):
        return self.points // LANES

    @property
    def tiles(self):
        return (self.span + self.taps - 1) * self.halves

    @property
    def per_pol(self):
        return self.devices // self.pols

    @property
    def half(self):
        return self.extent // 2

    @property
    def share(self):
        return self.beams // self.wide

    @property
    def local(self):
        return self.wide * self.per_device

    @property
    def all_bins(self):
        return self.spectra // INTEG

    @property
    def reach(self):
        return (BAND + self.extent - 1) * self.bins

    @property
    def lanes(self):
        return -(-self.reach // LANES) * LANES

    @property
    def shifts(self):
        return -(-(2 * self.all_bins - self.bins) // 8) * 8


def fourier_rows(points, owner_of):
    column = np.arange(points)
    phase_index = owner_of(column)[:, None] * column[None, :] % points
    angles = phase_index * (2.0 * np.pi / points)
    cosine = np.cos(angles) / np.sqrt(points)
    sine_part = np.sin(angles) / np.sqrt(points)
    real_row = np.concatenate([cosine, sine_part], axis=1)
    imag_row = np.concatenate([-sine_part, cosine], axis=1)
    table = np.concatenate([real_row, imag_row], axis=0).astype(np.float32)
    high = table.astype(jnp.bfloat16)
    return np.stack([high, (table - high.astype(np.float32)).astype(jnp.bfloat16)])


def one_hot(shape, matches):
    row = lax.broadcasted_iota(jnp.int32, shape, 0)
    column = lax.broadcasted_iota(jnp.int32, shape, 1)
    return matches(row, column).astype(jnp.float32)


def exact_dot(left, right, contract=(1, 0)):
    return lax.dot_general(
        left,
        right,
        (((contract[0],), (contract[1],)), ((), ())),
        precision=lax.Precision.HIGHEST,
        preferred_element_type=jnp.float32,
    )


def split(value):
    high = value.astype(jnp.bfloat16)
    return high, (value - high.astype(jnp.float32)).astype(jnp.bfloat16)


def fused_kernel(
    plan,
    taps_ref,
    smooth_ref,
    table_hbm,
    samples_ref,
    weights_ref,
    recv_ref,
    out_ref,
    table_ref,
    raw_ref,
    window_ref,
    stage_ref,
    send_ref,
    weight_ref,
    land_ref,
    energy_ref,
    shifted_ref,
    matrix_ref,
    outgoing_ref,
    gather_ref,
    raw_sem,
    table_sem,
    weight_sem,
    send_sem,
    recv_sem,
    last_sem,
    land_sem,
    share_sem,
    gather_sem,
    up_sem,
    down_sem,
    low_sem,
    high_sem,
):
    span, rows, groups, halves = plan.span, plan.rows, plan.groups, plan.halves
    tap_count, points, chunks = plan.taps, plan.points, plan.chunks
    my_wide = lax.axis_index("wide")
    my_narrow = lax.axis_index("narrow")
    me = my_wide * plan.narrow + my_narrow

    def peer(step):
        return (
            lax.rem(my_wide + step // plan.narrow, plan.wide),
            lax.rem(my_narrow + step % plan.narrow, plan.narrow),
        )

    def load_raw(chunk, slot):
        @pl.loop(0, plan.tiles)
        def _(tile):
            column = pl.multiple_of((chunk * span * halves + tile) * LANES, LANES)
            pltpu.make_async_copy(
                samples_ref.at[:, :, pl.ds(column, LANES)], raw_ref.at[slot, tile], raw_sem.at[slot]
            ).start()

    last = chunks - 1
    own_start = plan.half * plan.bins
    own_rows = plan.local * plan.bins
    part_rows = plan.per_device * plan.bins

    barrier = pltpu.get_barrier_semaphore()
    load_raw(0, 0)
    pltpu.make_async_copy(table_hbm, table_ref, table_sem).start()

    @pl.loop(1, plan.devices)
    def _(step):
        pl.semaphore_signal(barrier, inc=1, device_id=peer(step), device_id_type=MESH)

    @pl.loop(0, plan.per_device)
    def _(channel):
        pltpu.make_async_copy(
            weights_ref.at[channel], weight_ref.at[channel], weight_sem
        ).start()

    out_ref[...] = jnp.zeros_like(out_ref)

    def clear(start):
        gather_ref[:, start : start + own_start] = jnp.zeros(
            (chunks, own_start, plan.share), jnp.bfloat16
        )

    @pl.when(my_narrow == 0)
    def _():
        clear(0)

    @pl.when(my_narrow == plan.narrow - 1)
    def _():
        clear(own_start + own_rows)

    def filter_rows(slot):
        row_groups = 2 * plan.inputs // 8

        @pl.loop(0, halves * row_groups)
        def _(index):
            half = index // row_groups
            group = index % row_groups
            columns = pl.ds(pl.multiple_of(half * LANES, LANES), LANES)
            coeffs = [
                jnp.broadcast_to(taps_ref[tap : tap + 1, columns], (8, LANES))
                for tap in range(tap_count)
            ]
            sums = {}
            for frame in range(span + tap_count - 1):
                piece = raw_ref[slot, frame * halves + half, pl.ds(group * 4, 4)]
                value = piece.reshape(8, LANES).astype(jnp.float32)
                for out in range(max(0, frame - tap_count + 1), min(span - 1, frame) + 1):
                    term = coeffs[frame - out] * value
                    sums[out] = sums[out] + term if out in sums else term
                done = frame - tap_count + 1
                if done >= 0:
                    base = group * (8 * span) + done
                    window_ref[half, pl.ds(base, 8, stride=span), :] = sums.pop(done)

    def transform(slot):
        lane = lax.broadcasted_iota(jnp.int32, (points, LANES), 1)
        first = lane % (2 * span) < span
        product = functools.partial(
            lax.dot_general,
            dimension_numbers=(((1,), (1,)), ((), ())),
            preferred_element_type=jnp.float32,
        )
        pairs = 2

        @pl.loop(0, rows // (2 * pairs))
        def _(step):
            pieces = []
            for pair in range(pairs):
                for group in range(groups):
                    for member in range(2):
                        source = group * rows + step * (2 * pairs) + 2 * pair + member
                        blocks = []
                        for part in range(2):
                            start = pl.multiple_of((2 * source + part) * span, span)
                            for half in range(halves):
                                blocks.append(window_ref[half, pl.ds(start, span), :])
                        pieces.append(jnp.concatenate(blocks, axis=1))
            high, low = split(jnp.concatenate(pieces, axis=0))
            result = (
                product(table_ref[1], high)
                + product(table_ref[0], low)
                + product(table_ref[0], high)
            )
            for pair in range(pairs):
                real = result[:points, pair * LANES : (pair + 1) * LANES]
                imag = result[points:, pair * LANES : (pair + 1) * LANES]
                row = step * (2 * pairs) + 2 * pair
                stage_ref[pl.ds(row, points, stride=rows), :] = jnp.where(
                    first, real, pltpu.roll(imag, span, 1)
                )
                stage_ref[pl.ds(row + 1, points, stride=rows), :] = jnp.where(
                    first, pltpu.roll(real, LANES - span, 1), imag
                )

        send_ref[slot] = stage_ref[...].reshape(points, rows, LANES).astype(jnp.bfloat16)

    def start_sends(chunk, slot):
        @pl.loop(1, plan.devices)
        def _(step):
            wide, narrow = peer(step)
            target = wide * plan.narrow + narrow
            pltpu.make_async_remote_copy(
                src_ref=send_ref.at[slot, pl.ds(target * plan.per_device, plan.per_device)],
                dst_ref=recv_ref.at[chunk, me],
                send_sem=send_sem.at[slot],
                recv_sem=recv_sem.at[chunk],
                device_id=(wide, narrow),
                device_id_type=MESH,
            ).start()

        pltpu.make_async_copy(
            send_ref.at[slot, pl.ds(me * plan.per_device, plan.per_device)],
            recv_ref.at[chunk, me],
            recv_sem.at[chunk],
        ).start()

    def start_last(index, slot):
        def voltages(target):
            first = target * plan.per_device + index * plan.together
            return send_ref.at[slot, pl.ds(first, plan.together)]

        landing = land_ref.at[1, me, pl.ds(index * plan.together, plan.together)]

        @pl.loop(1, plan.devices)
        def _(step):
            wide, narrow = peer(step)
            pltpu.make_async_remote_copy(
                src_ref=voltages(wide * plan.narrow + narrow),
                dst_ref=landing,
                send_sem=send_sem.at[slot],
                recv_sem=last_sem.at[index],
                device_id=(wide, narrow),
                device_id_type=MESH,
            ).start()

        pltpu.make_async_copy(voltages(me), landing, last_sem.at[index]).start()

    def wait_sends(slot):
        sent = send_ref.at[slot, pl.ds(0, (plan.devices - 1) * plan.per_device)]
        pltpu.make_async_copy(sent, sent, send_sem.at[slot]).wait()

    def form_beams(chunk):
        together = plan.together
        landed = (chunk == last).astype(jnp.int32)

        @pl.when(chunk < last)
        def _():
            arrived = recv_ref.at[chunk]
            pltpu.make_async_copy(arrived, arrived, recv_sem.at[chunk]).wait()
            landing = pltpu.make_async_copy(arrived, land_ref.at[0], land_sem)
            landing.start()
            landing.wait()

        @pl.loop(0, plan.sets)
        def _(step):
            @pl.when((chunk == last) & (step == plan.sets - 1))
            def _():
                catch_up()

            @pl.when(chunk == last)
            def _():
                arrived = land_ref.at[1, :, pl.ds(step * together, together)]
                pltpu.make_async_copy(arrived, arrived, last_sem.at[step]).wait()

            binned = []
            for member in range(together):
                channel = step * together + member
                energy = None
                for pol in range(plan.pols):
                    block = land_ref[landed, pol * plan.per_pol : (pol + 1) * plan.per_pol, channel]
                    block = block.astype(jnp.float32).reshape(plan.per_pol * rows, LANES)
                    turned = block.T.astype(jnp.bfloat16)
                    formed = None
                    for group in range(groups):
                        base = 2 * span * group
                        straight = turned[base : base + 2 * span]
                        crossed = jnp.concatenate(
                            [-straight[span:], straight[:span]], axis=0
                        )
                        for side, left in enumerate((straight, crossed)):
                            right = weight_ref[channel, pol, side, :, group]
                            right = right.reshape(-1, plan.beams)
                            term = jnp.dot(left, right, preferred_element_type=jnp.float32)
                            formed = term if formed is None else formed + term
                    squares = formed * formed
                    power = squares[:span] + squares[span:]
                    energy = power if energy is None else energy + power
                binned.append(energy.reshape(plan.bins, INTEG, plan.beams).sum(axis=1))
            energy_ref[pl.ds(pl.multiple_of(step * 8, 8), 8), :] = jnp.concatenate(
                binned, axis=0
            )

        scale = jnp.float32(1.0 / (plan.pols * INTEG))
        intensity = (energy_ref[...] * scale).astype(jnp.bfloat16)
        for owner in range(plan.wide):
            outgoing_ref[chunk, owner] = intensity[:, owner * plan.share : (owner + 1) * plan.share]

        mine = pl.ds(pl.multiple_of(own_start + my_wide * part_rows, part_rows), part_rows)

        @pl.loop(1, plan.wide)
        def _(step):
            target = lax.rem(my_wide + step, plan.wide)
            pltpu.make_async_remote_copy(
                src_ref=outgoing_ref.at[chunk, target],
                dst_ref=gather_ref.at[chunk, mine],
                send_sem=share_sem.at[chunk],
                recv_sem=gather_sem.at[chunk],
                device_id=(target, my_narrow),
                device_id_type=MESH,
            ).start()

        pltpu.make_async_copy(
            outgoing_ref.at[chunk, my_wide], gather_ref.at[chunk, mine], gather_sem.at[chunk]
        ).start()

    def halo(chunk):
        def upward():
            return pltpu.make_async_remote_copy(
                src_ref=gather_ref.at[chunk, pl.ds(own_rows, own_start)],
                dst_ref=gather_ref.at[chunk, pl.ds(0, own_start)],
                send_sem=up_sem.at[chunk],
                recv_sem=low_sem.at[chunk],
                device_id=(my_wide, my_narrow + 1),
                device_id_type=MESH,
            )

        def downward():
            return pltpu.make_async_remote_copy(
                src_ref=gather_ref.at[chunk, pl.ds(own_start, own_start)],
                dst_ref=gather_ref.at[chunk, pl.ds(own_start + own_rows, own_start)],
                send_sem=down_sem.at[chunk],
                recv_sem=high_sem.at[chunk],
                device_id=(my_wide, my_narrow - 1),
                device_id_type=MESH,
            )

        return upward, downward

    def start_halo(chunk):
        own = gather_ref.at[chunk, pl.ds(own_start, own_rows)]
        pltpu.make_async_copy(own, own, gather_sem.at[chunk]).wait()
        upward, downward = halo(chunk)

        @pl.when(my_narrow < plan.narrow - 1)
        def _():
            upward().start()

        @pl.when(my_narrow > 0)
        def _():
            downward().start()

    def build_matrix():
        extent, bins, shifts, lanes = plan.extent, plan.bins, plan.shifts, plan.lanes
        last = plan.all_bins - bins
        spread = one_hot((extent, lanes), lambda row, column: row == column // bins)
        columns = exact_dot(smooth_ref[...], spread, (0, 0))
        inner = lax.broadcasted_iota(jnp.int32, (shifts, lanes), 1) % bins
        shifted = jnp.zeros((shifts, lanes), jnp.float32)
        for offset in range(bins):
            select = one_hot(
                (shifts, extent),
                lambda row, column: column == offset - row + last + plan.half,
            )
            shifted = jnp.where(inner == offset, exact_dot(select, columns), shifted)
        shifted_ref[...] = shifted
        gather = one_hot(
            (plan.all_bins, shifts),
            lambda row, column: (column >= row)
            & (column <= row + last)
            & ((column - row) % bins == 0),
        )
        block = one_hot((lanes, lanes), lambda row, column: row // bins == column // bins)
        total = exact_dot(exact_dot(gather, shifted), block)
        mean = total * jnp.float32(1.0 / plan.all_bins)

        @pl.loop(0, chunks)
        def _(chunk):
            start = shifts - (last - bins * chunk)
            rows_here = pltpu.roll(shifted_ref[...], lax.rem(start, shifts), 0)[: plan.all_bins]
            centered = rows_here - mean
            for channel in range(BAND):
                moved = pltpu.roll(centered, bins * channel, 1) if channel else centered
                place = slice(channel * plan.all_bins, (channel + 1) * plan.all_bins)
                matrix_ref[chunk, 0, place], matrix_ref[chunk, 1, place] = split(moved)

    def smooth(chunk):
        upward, downward = halo(chunk)

        @pl.when(my_narrow > 0)
        def _():
            upward().wait_recv()

        @pl.when(my_narrow < plan.narrow - 1)
        def _():
            downward().wait_recv()

        for band in range(plan.local // BAND):
            start = band * BAND * plan.bins
            values = gather_ref[chunk, start : start + plan.reach]
            size = BAND * plan.all_bins
            place = slice(band * size, (band + 1) * size)
            total = out_ref[place]
            for side in (1, 0):
                total = total + jnp.dot(
                    matrix_ref[chunk, side, :, : plan.reach],
                    values,
                    preferred_element_type=jnp.float32,
                )
            out_ref[place] = total

    def catch_up():
        start_halo(last - 2)
        smooth(last - 3)
        start_halo(last - 1)
        smooth(last - 2)

    @pl.loop(0, chunks + LAG)
    def _(step):
        @pl.when(step < chunks)
        def _():
            side = step % 2
            slot = step % SLOTS
            raw = raw_ref.at[side]
            pltpu.make_async_copy(raw, raw, raw_sem.at[side]).wait()

            @pl.when(step + 1 < chunks)
            def _():
                load_raw(step + 1, 1 - side)

            filter_rows(side)

            @pl.when(step >= SLOTS)
            def _():
                wait_sends(slot)

            @pl.when(step == 0)
            def _():
                pltpu.make_async_copy(table_hbm, table_ref, table_sem).wait()

            transform(slot)

            @pl.when(step == 0)
            def _():
                pl.semaphore_wait(barrier, plan.devices - 1)

            @pl.when(step < last)
            def _():
                start_sends(step, slot)

            @pl.when(step == last)
            def _():
                @pl.loop(0, plan.sets - 1)
                def _(index):
                    start_last(index, slot)

        @pl.when(step == LAG)
        def _():
            build_matrix()
            pltpu.make_async_copy(weight_ref, weight_ref, weight_sem).wait()

        @pl.when(step >= LAG)
        def _():
            form_beams(step - LAG)

        @pl.when(step == last + 1)
        def _():
            start_last(plan.sets - 1, last % SLOTS)

        @pl.when((step >= HALO_LAG) & (step <= last + 1))
        def _():
            start_halo(step - HALO_LAG)

        @pl.when((step >= SMOOTH_LAG) & (step <= last + 1))
        def _():
            smooth(step - SMOOTH_LAG)

    smooth(last - 1)
    start_halo(last)
    smooth(last)

    for slot in range(min(SLOTS, chunks)):
        wait_sends(slot)

    @pl.loop(0, chunks)
    def _(chunk):
        sent = outgoing_ref.at[chunk, pl.ds(0, plan.wide - 1)]
        pltpu.make_async_copy(sent, sent, share_sem.at[chunk]).wait()
        upward, downward = halo(chunk)

        @pl.when(my_narrow < plan.narrow - 1)
        def _():
            upward().wait_send()

        @pl.when(my_narrow > 0)
        def _():
            downward().wait_send()


def fused(samples, filter_taps, table, beam_weights, smooth_kernel, plan):
    if plan.groups == 1:
        dish_split = (1, 1, plan.dishes)
    else:
        dish_split = (plan.per_pol, plan.groups, plan.rows)
    weight_shape = (plan.per_device, plan.pols, 2, *dish_split, plan.beams)
    weights = beam_weights.reshape(weight_shape)
    anywhere = pl.BlockSpec(memory_space=pl.ANY)
    local = pl.BlockSpec(memory_space=pltpu.VMEM)
    recv_shape = (plan.chunks - 1, plan.devices, plan.per_device, plan.rows, LANES)
    energy_shape = (plan.per_device * plan.bins, plan.beams)
    ext_rows = (plan.local + 2 * plan.half) * plan.bins
    out_shape = (plan.local * plan.all_bins, plan.share)
    per_chunk = pltpu.SemaphoreType.DMA((plan.chunks,))
    return pl.pallas_call(
        functools.partial(fused_kernel, plan),
        in_specs=[local, local, anywhere, anywhere, anywhere],
        out_specs=[anywhere, local],
        out_shape=[
            jax.ShapeDtypeStruct(recv_shape, jnp.bfloat16),
            jax.ShapeDtypeStruct(out_shape, jnp.float32),
        ],
        scratch_shapes=[
            pltpu.VMEM(table.shape, jnp.bfloat16),
            pltpu.VMEM((2, plan.tiles, plan.inputs, 2, LANES), jnp.bfloat16),
            pltpu.VMEM((plan.halves, 2 * plan.inputs * plan.span, LANES), jnp.float32),
            pltpu.VMEM((plan.points * plan.rows, LANES), jnp.float32),
            pltpu.VMEM((SLOTS, plan.points, plan.rows, LANES), jnp.bfloat16),
            pltpu.VMEM(weight_shape, jnp.bfloat16),
            pltpu.VMEM((2, *recv_shape[1:]), jnp.bfloat16),
            pltpu.VMEM(energy_shape, jnp.float32),
            pltpu.VMEM((plan.shifts, plan.lanes), jnp.float32),
            pltpu.VMEM((plan.chunks, 2, BAND * plan.all_bins, plan.lanes), jnp.bfloat16),
            pltpu.VMEM(
                (plan.chunks, plan.wide, plan.per_device * plan.bins, plan.share), jnp.bfloat16
            ),
            pltpu.VMEM((plan.chunks, ext_rows, plan.share), jnp.bfloat16),
            pltpu.SemaphoreType.DMA((2,)),
            pltpu.SemaphoreType.DMA,
            pltpu.SemaphoreType.DMA,
            pltpu.SemaphoreType.DMA((SLOTS,)),
            per_chunk,
            pltpu.SemaphoreType.DMA((plan.sets,)),
            pltpu.SemaphoreType.DMA,
            *([per_chunk] * 6),
        ],
        compiler_params=pltpu.CompilerParams(
            collective_id=0, has_side_effects=True, vmem_limit_bytes=66 * 1000 * 1000
        ),
        name="fused",
    )(filter_taps, smooth_kernel, table, samples, weights)[1]


def body(samples, filter_taps, beam_weights, smooth_kernel):
    tap_count, points = filter_taps.shape
    wide_count = lax.axis_size("wide")
    narrow_count = lax.axis_size("narrow")
    per_device, pols, _, dishes, beams = beam_weights.shape
    frames = samples.shape[2] // points
    plan = Plan(
        wide=wide_count,
        narrow=narrow_count,
        inputs=samples.shape[0],
        per_device=per_device,
        points=points,
        taps=tap_count,
        pols=pols,
        dishes=dishes,
        beams=beams,
        spectra=frames - tap_count + 1,
        extent=smooth_kernel.shape[0],
    )

    def owner_of(column):
        device_slot = column // per_device
        return (
            device_slot % narrow_count * wide_count + device_slot // narrow_count
        ) * per_device + column % per_device

    table = jnp.asarray(fourier_rows(points, owner_of))
    filtered = fused(samples, filter_taps, table, beam_weights, smooth_kernel, plan)
    return filtered.reshape(plan.local, plan.all_bins, plan.share)


def solution(mesh):
    placed = (
        P(("wide", "narrow"), None, None),
        P(),
        P(("narrow", "wide"), None, None, None, None),
        P(),
    )
    return jax.shard_map(
        body, mesh=mesh, in_specs=placed, out_specs=P("narrow", None, "wide"), check_vma=False
    )
```

```python
import dataclasses
import functools

import jax
import jax.numpy as jnp
import numpy as np
from jax import lax
from jax.experimental import pallas as pl
from jax.experimental.pallas import tpu as pltpu
from jax.sharding import PartitionSpec as P

INTEG = 8
LANES = 128
BAND = 8
SLOTS = 3
LAG = 2
PAIRS = 2
HALO_LAG = 4
SMOOTH_LAG = 5
MESH = pl.DeviceIdType.MESH


@dataclasses.dataclass(frozen=True)
class Plan:
    wide: int
    narrow: int
    inputs: int
    per_device: int
    points: int
    taps: int
    pols: int
    dishes: int
    beams: int
    spectra: int
    extent: int

    @property
    def devices(self):
        return self.wide * self.narrow

    @property
    def groups(self):
        return max(1, self.inputs // 16)

    @property
    def rows(self):
        return self.inputs // self.groups

    @property
    def span(self):
        return LANES // (2 * self.groups)

    @property
    def chunks(self):
        return self.spectra // self.span

    @property
    def bins(self):
        return self.span // INTEG

    @property
    def turns(self):
        return self.rows // (2 * PAIRS)

    @property
    def together(self):
        return 8 // self.bins

    @property
    def sets(self):
        return self.per_device // self.together

    @property
    def halves(self):
        return self.points // LANES

    @property
    def tiles(self):
        return (self.span + self.taps - 1) * self.halves

    @property
    def per_pol(self):
        return self.devices // self.pols

    @property
    def half(self):
        return self.extent // 2

    @property
    def share(self):
        return self.beams // self.wide

    @property
    def local(self):
        return self.wide * self.per_device

    @property
    def all_bins(self):
        return self.spectra // INTEG

    @property
    def reach(self):
        return (BAND + self.extent - 1) * self.bins

    @property
    def lanes(self):
        return -(-self.reach // LANES) * LANES

    @property
    def shifts(self):
        return -(-(2 * self.all_bins - self.bins) // 8) * 8


def fourier_rows(points, owner_of, blocks):
    column = np.arange(points)
    phase_index = owner_of(column)[:, None] * column[None, :] % points
    angles = phase_index * (2.0 * np.pi / points)
    cosine = np.cos(angles) / np.sqrt(points)
    sine_part = np.sin(angles) / np.sqrt(points)
    real_row = np.concatenate([cosine, sine_part], axis=1)
    imag_row = np.concatenate([-sine_part, cosine], axis=1)
    table = np.stack([part.reshape(blocks, -1, 2 * points) for part in (real_row, imag_row)], axis=1)
    table = table.reshape(2 * points, 2 * points).astype(np.float32)
    high = table.astype(jnp.bfloat16)
    return np.stack([high, (table - high.astype(np.float32)).astype(jnp.bfloat16)])


def one_hot(shape, matches):
    row = lax.broadcasted_iota(jnp.int32, shape, 0)
    column = lax.broadcasted_iota(jnp.int32, shape, 1)
    return matches(row, column).astype(jnp.float32)


def exact_dot(left, right, contract=(1, 0)):
    return lax.dot_general(
        left,
        right,
        (((contract[0],), (contract[1],)), ((), ())),
        precision=lax.Precision.HIGHEST,
        preferred_element_type=jnp.float32,
    )


def split(value):
    high = value.astype(jnp.bfloat16)
    return high, (value - high.astype(jnp.float32)).astype(jnp.bfloat16)


def fused_kernel(
    plan,
    taps_ref,
    smooth_ref,
    table_hbm,
    samples_ref,
    weights_ref,
    recv_ref,
    out_ref,
    table_ref,
    raw_ref,
    window_ref,
    signal_ref,
    stage_ref,
    send_ref,
    weight_ref,
    land_ref,
    energy_ref,
    shifted_ref,
    matrix_ref,
    outgoing_ref,
    gather_ref,
    raw_sem,
    table_sem,
    weight_sem,
    send_sem,
    recv_sem,
    last_sem,
    land_sem,
    share_sem,
    gather_sem,
    up_sem,
    down_sem,
    low_sem,
    high_sem,
):
    span, rows, groups, halves = plan.span, plan.rows, plan.groups, plan.halves
    tap_count, points, chunks = plan.taps, plan.points, plan.chunks
    my_wide = lax.axis_index("wide")
    my_narrow = lax.axis_index("narrow")
    me = my_wide * plan.narrow + my_narrow

    def peer(step):
        return (
            lax.rem(my_wide + step // plan.narrow, plan.wide),
            lax.rem(my_narrow + step % plan.narrow, plan.narrow),
        )

    def load_raw(chunk, slot):
        @pl.loop(0, plan.tiles)
        def _(tile):
            column = pl.multiple_of((chunk * span * halves + tile) * LANES, LANES)
            pltpu.make_async_copy(
                samples_ref.at[:, :, pl.ds(column, LANES)], raw_ref.at[slot, tile], raw_sem.at[slot]
            ).start()

    last = chunks - 1
    own_start = plan.half * plan.bins
    own_rows = plan.local * plan.bins
    part_rows = plan.per_device * plan.bins

    barrier = pltpu.get_barrier_semaphore()
    load_raw(0, 0)
    pltpu.make_async_copy(table_hbm, table_ref, table_sem).start()

    @pl.loop(1, plan.devices)
    def _(step):
        pl.semaphore_signal(barrier, inc=1, device_id=peer(step), device_id_type=MESH)

    @pl.loop(0, plan.per_device)
    def _(channel):
        pltpu.make_async_copy(
            weights_ref.at[channel], weight_ref.at[channel], weight_sem
        ).start()

    out_ref[...] = jnp.zeros_like(out_ref)

    def clear(start):
        gather_ref[:, start : start + own_start] = jnp.zeros(
            (chunks, own_start, plan.share), jnp.bfloat16
        )

    @pl.when(my_narrow == 0)
    def _():
        clear(0)

    @pl.when(my_narrow == plan.narrow - 1)
    def _():
        clear(own_start + own_rows)

    def filter_rows(slot):
        row_groups = 2 * plan.inputs // 8

        @pl.loop(0, halves * row_groups)
        def _(index):
            half = index // row_groups
            group = index % row_groups
            columns = pl.ds(pl.multiple_of(half * LANES, LANES), LANES)
            coeffs = [
                jnp.broadcast_to(taps_ref[tap : tap + 1, columns], (8, LANES))
                for tap in range(tap_count)
            ]
            sums = {}
            for frame in range(span + tap_count - 1):
                piece = raw_ref[slot, frame * halves + half, pl.ds(group * 4, 4)]
                value = piece.reshape(8, LANES).astype(jnp.float32)
                for out in range(max(0, frame - tap_count + 1), min(span - 1, frame) + 1):
                    term = coeffs[frame - out] * value
                    sums[out] = sums[out] + term if out in sums else term
                done = frame - tap_count + 1
                if done >= 0:
                    base = group * (8 * span) + done
                    window_ref[half, pl.ds(base, 8, stride=span), :] = sums.pop(done)

    def prepare():
        @pl.loop(0, plan.turns)
        def _(step):
            pieces = []
            for pair in range(PAIRS):
                for group in range(groups):
                    for member in range(2):
                        source = group * rows + step * (2 * PAIRS) + 2 * pair + member
                        blocks = []
                        for part in range(2):
                            start = pl.multiple_of((2 * source + part) * span, span)
                            for half in range(halves):
                                blocks.append(window_ref[half, pl.ds(start, span), :])
                        pieces.append(jnp.concatenate(blocks, axis=1))
            signal_ref[0, step], signal_ref[1, step] = split(jnp.concatenate(pieces, axis=0))

    def transform(block, slot):
        channels = plan.narrow * plan.per_device
        lane = lax.broadcasted_iota(jnp.int32, (channels, LANES), 1)
        first = lane % (2 * span) < span
        product = functools.partial(
            lax.dot_general,
            dimension_numbers=(((1,), (1,)), ((), ())),
            preferred_element_type=jnp.float32,
        )
        table_rows = pl.ds(pl.multiple_of(block * (2 * channels), 2 * channels), 2 * channels)

        @pl.loop(0, plan.turns)
        def _(step):
            high, low = signal_ref[0, step], signal_ref[1, step]
            result = (
                product(table_ref[1, table_rows], high)
                + product(table_ref[0, table_rows], low)
                + product(table_ref[0, table_rows], high)
            )
            for pair in range(PAIRS):
                real = result[:channels, pair * LANES : (pair + 1) * LANES]
                imag = result[channels:, pair * LANES : (pair + 1) * LANES]
                row = step * (2 * PAIRS) + 2 * pair
                stage_ref[pl.ds(row, channels, stride=rows), :] = jnp.where(
                    first, real, pltpu.roll(imag, span, 1)
                )
                stage_ref[pl.ds(row + 1, channels, stride=rows), :] = jnp.where(
                    first, pltpu.roll(real, LANES - span, 1), imag
                )

        place = pl.ds(pl.multiple_of(block * channels, channels), channels)
        send_ref[slot, place] = (
            stage_ref[...].reshape(channels, rows, LANES).astype(jnp.bfloat16)
        )

    def block_at(step):
        moved = lax.rem(step + plan.wide // 2, plan.wide)
        if plan.wide & (plan.wide - 1) == 0:
            return lax.bitwise_xor(my_wide, moved)
        return lax.rem(my_wide + moved, plan.wide)

    def start_sends(chunk, block, slot):
        @pl.loop(0, plan.narrow)
        def _(step):
            narrow = lax.rem(my_narrow + step, plan.narrow)
            target = block * plan.narrow + narrow
            source = send_ref.at[slot, pl.ds(target * plan.per_device, plan.per_device)]

            @pl.when(target != me)
            def _():
                pltpu.make_async_remote_copy(
                    src_ref=source,
                    dst_ref=recv_ref.at[chunk, me],
                    send_sem=send_sem.at[slot],
                    recv_sem=recv_sem.at[chunk],
                    device_id=(block, narrow),
                    device_id_type=MESH,
                ).start()

            @pl.when(target == me)
            def _():
                pltpu.make_async_copy(source, recv_ref.at[chunk, me], recv_sem.at[chunk]).start()

    def start_last(index, slot):
        def voltages(target):
            first = target * plan.per_device + index * plan.together
            return send_ref.at[slot, pl.ds(first, plan.together)]

        landing = land_ref.at[1, me, pl.ds(index * plan.together, plan.together)]

        @pl.loop(1, plan.devices)
        def _(step):
            wide, narrow = peer(step)
            pltpu.make_async_remote_copy(
                src_ref=voltages(wide * plan.narrow + narrow),
                dst_ref=landing,
                send_sem=send_sem.at[slot],
                recv_sem=last_sem.at[index],
                device_id=(wide, narrow),
                device_id_type=MESH,
            ).start()

        pltpu.make_async_copy(voltages(me), landing, last_sem.at[index]).start()

    def wait_sends(slot):
        sent = send_ref.at[slot, pl.ds(0, (plan.devices - 1) * plan.per_device)]
        pltpu.make_async_copy(sent, sent, send_sem.at[slot]).wait()

    def form_beams(chunk):
        together = plan.together
        landed = (chunk == last).astype(jnp.int32)

        @pl.when(chunk < last)
        def _():
            arrived = recv_ref.at[chunk]
            pltpu.make_async_copy(arrived, arrived, recv_sem.at[chunk]).wait()
            landing = pltpu.make_async_copy(arrived, land_ref.at[0], land_sem)
            landing.start()
            landing.wait()

        @pl.loop(0, plan.sets)
        def _(step):
            @pl.when((chunk == last) & (step == plan.sets - 1))
            def _():
                catch_up()

            @pl.when(chunk == last)
            def _():
                arrived = land_ref.at[1, :, pl.ds(step * together, together)]
                pltpu.make_async_copy(arrived, arrived, last_sem.at[step]).wait()

            binned = []
            for member in range(together):
                channel = step * together + member
                energy = None
                for pol in range(plan.pols):
                    block = land_ref[landed, pol * plan.per_pol : (pol + 1) * plan.per_pol, channel]
                    block = block.astype(jnp.float32).reshape(plan.per_pol * rows, LANES)
                    turned = block.T.astype(jnp.bfloat16)
                    formed = None
                    for group in range(groups):
                        base = 2 * span * group
                        straight = turned[base : base + 2 * span]
                        crossed = jnp.concatenate(
                            [-straight[span:], straight[:span]], axis=0
                        )
                        for side, left in enumerate((straight, crossed)):
                            right = weight_ref[channel, pol, side, :, group]
                            right = right.reshape(-1, plan.beams)
                            term = jnp.dot(left, right, preferred_element_type=jnp.float32)
                            formed = term if formed is None else formed + term
                    squares = formed * formed
                    power = squares[:span] + squares[span:]
                    energy = power if energy is None else energy + power
                binned.append(energy.reshape(plan.bins, INTEG, plan.beams).sum(axis=1))
            energy_ref[pl.ds(pl.multiple_of(step * 8, 8), 8), :] = jnp.concatenate(
                binned, axis=0
            )

        scale = jnp.float32(1.0 / (plan.pols * INTEG))
        intensity = (energy_ref[...] * scale).astype(jnp.bfloat16)
        for owner in range(plan.wide):
            outgoing_ref[chunk, owner] = intensity[:, owner * plan.share : (owner + 1) * plan.share]

        mine = pl.ds(pl.multiple_of(own_start + my_wide * part_rows, part_rows), part_rows)

        @pl.loop(1, plan.wide)
        def _(step):
            target = lax.rem(my_wide + step, plan.wide)
            pltpu.make_async_remote_copy(
                src_ref=outgoing_ref.at[chunk, target],
                dst_ref=gather_ref.at[chunk, mine],
                send_sem=share_sem.at[chunk],
                recv_sem=gather_sem.at[chunk],
                device_id=(target, my_narrow),
                device_id_type=MESH,
            ).start()

        pltpu.make_async_copy(
            outgoing_ref.at[chunk, my_wide], gather_ref.at[chunk, mine], gather_sem.at[chunk]
        ).start()

    def halo(chunk):
        def upward():
            return pltpu.make_async_remote_copy(
                src_ref=gather_ref.at[chunk, pl.ds(own_rows, own_start)],
                dst_ref=gather_ref.at[chunk, pl.ds(0, own_start)],
                send_sem=up_sem.at[chunk],
                recv_sem=low_sem.at[chunk],
                device_id=(my_wide, my_narrow + 1),
                device_id_type=MESH,
            )

        def downward():
            return pltpu.make_async_remote_copy(
                src_ref=gather_ref.at[chunk, pl.ds(own_start, own_start)],
                dst_ref=gather_ref.at[chunk, pl.ds(own_start + own_rows, own_start)],
                send_sem=down_sem.at[chunk],
                recv_sem=high_sem.at[chunk],
                device_id=(my_wide, my_narrow - 1),
                device_id_type=MESH,
            )

        return upward, downward

    def start_halo(chunk):
        own = gather_ref.at[chunk, pl.ds(own_start, own_rows)]
        pltpu.make_async_copy(own, own, gather_sem.at[chunk]).wait()
        upward, downward = halo(chunk)

        @pl.when(my_narrow < plan.narrow - 1)
        def _():
            upward().start()

        @pl.when(my_narrow > 0)
        def _():
            downward().start()

    def build_matrix():
        extent, bins, shifts, lanes = plan.extent, plan.bins, plan.shifts, plan.lanes
        last = plan.all_bins - bins
        spread = one_hot((extent, lanes), lambda row, column: row == column // bins)
        columns = exact_dot(smooth_ref[...], spread, (0, 0))
        inner = lax.broadcasted_iota(jnp.int32, (shifts, lanes), 1) % bins
        shifted = jnp.zeros((shifts, lanes), jnp.float32)
        for offset in range(bins):
            select = one_hot(
                (shifts, extent),
                lambda row, column: column == offset - row + last + plan.half,
            )
            shifted = jnp.where(inner == offset, exact_dot(select, columns), shifted)
        shifted_ref[...] = shifted
        gather = one_hot(
            (plan.all_bins, shifts),
            lambda row, column: (column >= row)
            & (column <= row + last)
            & ((column - row) % bins == 0),
        )
        block = one_hot((lanes, lanes), lambda row, column: row // bins == column // bins)
        total = exact_dot(exact_dot(gather, shifted), block)
        mean = total * jnp.float32(1.0 / plan.all_bins)

        @pl.loop(0, chunks)
        def _(chunk):
            start = shifts - (last - bins * chunk)
            rows_here = pltpu.roll(shifted_ref[...], lax.rem(start, shifts), 0)[: plan.all_bins]
            centered = rows_here - mean
            for channel in range(BAND):
                moved = pltpu.roll(centered, bins * channel, 1) if channel else centered
                place = slice(channel * plan.all_bins, (channel + 1) * plan.all_bins)
                matrix_ref[chunk, 0, place], matrix_ref[chunk, 1, place] = split(moved)

    def smooth(chunk):
        upward, downward = halo(chunk)

        @pl.when(my_narrow > 0)
        def _():
            upward().wait_recv()

        @pl.when(my_narrow < plan.narrow - 1)
        def _():
            downward().wait_recv()

        for band in range(plan.local // BAND):
            start = band * BAND * plan.bins
            values = gather_ref[chunk, start : start + plan.reach]
            size = BAND * plan.all_bins
            place = slice(band * size, (band + 1) * size)
            total = out_ref[place]
            for side in (1, 0):
                total = total + jnp.dot(
                    matrix_ref[chunk, side, :, : plan.reach],
                    values,
                    preferred_element_type=jnp.float32,
                )
            out_ref[place] = total

    def catch_up():
        start_halo(last - 2)
        smooth(last - 3)
        start_halo(last - 1)
        smooth(last - 2)

    @pl.loop(0, chunks + LAG)
    def _(step):
        @pl.when(step < chunks)
        def _():
            side = step % 2
            slot = step % SLOTS
            raw = raw_ref.at[side]
            pltpu.make_async_copy(raw, raw, raw_sem.at[side]).wait()

            @pl.when(step + 1 < chunks)
            def _():
                load_raw(step + 1, 1 - side)

            filter_rows(side)

            @pl.when(step >= SLOTS)
            def _():
                wait_sends(slot)

            @pl.when(step == 0)
            def _():
                pltpu.make_async_copy(table_hbm, table_ref, table_sem).wait()

            prepare()

            @pl.loop(0, plan.wide)
            def _(turn):
                block = block_at(turn)
                transform(block, slot)

                @pl.when((step == 0) & (turn == 0))
                def _():
                    pl.semaphore_wait(barrier, plan.devices - 1)

                @pl.when(step < last)
                def _():
                    start_sends(step, block, slot)

            @pl.when(step == last)
            def _():
                @pl.loop(0, plan.sets - 1)
                def _(index):
                    start_last(index, slot)

        @pl.when(step == LAG)
        def _():
            build_matrix()
            pltpu.make_async_copy(weight_ref, weight_ref, weight_sem).wait()

        @pl.when(step >= LAG)
        def _():
            form_beams(step - LAG)

        @pl.when(step == last + 1)
        def _():
            start_last(plan.sets - 1, last % SLOTS)

        @pl.when((step >= HALO_LAG) & (step <= last + 1))
        def _():
            start_halo(step - HALO_LAG)

        @pl.when((step >= SMOOTH_LAG) & (step <= last + 1))
        def _():
            smooth(step - SMOOTH_LAG)

    smooth(last - 1)
    start_halo(last)
    smooth(last)

    for slot in range(min(SLOTS, chunks)):
        wait_sends(slot)

    @pl.loop(0, chunks)
    def _(chunk):
        sent = outgoing_ref.at[chunk, pl.ds(0, plan.wide - 1)]
        pltpu.make_async_copy(sent, sent, share_sem.at[chunk]).wait()
        upward, downward = halo(chunk)

        @pl.when(my_narrow < plan.narrow - 1)
        def _():
            upward().wait_send()

        @pl.when(my_narrow > 0)
        def _():
            downward().wait_send()


def fused(samples, filter_taps, table, beam_weights, smooth_kernel, plan):
    if plan.groups == 1:
        dish_split = (1, 1, plan.dishes)
    else:
        dish_split = (plan.per_pol, plan.groups, plan.rows)
    weight_shape = (plan.per_device, plan.pols, 2, *dish_split, plan.beams)
    weights = beam_weights.reshape(weight_shape)
    anywhere = pl.BlockSpec(memory_space=pl.ANY)
    local = pl.BlockSpec(memory_space=pltpu.VMEM)
    recv_shape = (plan.chunks - 1, plan.devices, plan.per_device, plan.rows, LANES)
    energy_shape = (plan.per_device * plan.bins, plan.beams)
    ext_rows = (plan.local + 2 * plan.half) * plan.bins
    out_shape = (plan.local * plan.all_bins, plan.share)
    per_chunk = pltpu.SemaphoreType.DMA((plan.chunks,))
    return pl.pallas_call(
        functools.partial(fused_kernel, plan),
        in_specs=[local, local, anywhere, anywhere, anywhere],
        out_specs=[anywhere, local],
        out_shape=[
            jax.ShapeDtypeStruct(recv_shape, jnp.bfloat16),
            pltpu.VMEM(out_shape, jnp.float32),
        ],
        scratch_shapes=[
            pltpu.VMEM(table.shape, jnp.bfloat16),
            pltpu.VMEM((2, plan.tiles, plan.inputs, 2, LANES), jnp.bfloat16),
            pltpu.VMEM((plan.halves, 2 * plan.inputs * plan.span, LANES), jnp.float32),
            pltpu.VMEM((2, plan.turns, 2 * PAIRS * plan.groups * plan.span, 2 * plan.points), jnp.bfloat16),
            pltpu.VMEM((plan.points // plan.wide * plan.rows, LANES), jnp.float32),
            pltpu.VMEM((SLOTS, plan.points, plan.rows, LANES), jnp.bfloat16),
            pltpu.VMEM(weight_shape, jnp.bfloat16),
            pltpu.VMEM((2, *recv_shape[1:]), jnp.bfloat16),
            pltpu.VMEM(energy_shape, jnp.float32),
            pltpu.VMEM((plan.shifts, plan.lanes), jnp.float32),
            pltpu.VMEM((plan.chunks, 2, BAND * plan.all_bins, plan.lanes), jnp.bfloat16),
            pltpu.VMEM(
                (plan.chunks, plan.wide, plan.per_device * plan.bins, plan.share), jnp.bfloat16
            ),
            pltpu.VMEM((plan.chunks, ext_rows, plan.share), jnp.bfloat16),
            pltpu.SemaphoreType.DMA((2,)),
            pltpu.SemaphoreType.DMA,
            pltpu.SemaphoreType.DMA,
            pltpu.SemaphoreType.DMA((SLOTS,)),
            per_chunk,
            pltpu.SemaphoreType.DMA((plan.sets,)),
            pltpu.SemaphoreType.DMA,
            *([per_chunk] * 6),
        ],
        compiler_params=pltpu.CompilerParams(
            collective_id=0, has_side_effects=True, vmem_limit_bytes=62 * 1000 * 1000
        ),
        name="fused",
    )(filter_taps, smooth_kernel, table, samples, weights)[1]


def body(samples, filter_taps, beam_weights, smooth_kernel):
    tap_count, points = filter_taps.shape
    wide_count = lax.axis_size("wide")
    narrow_count = lax.axis_size("narrow")
    per_device, pols, _, dishes, beams = beam_weights.shape
    frames = samples.shape[2] // points
    plan = Plan(
        wide=wide_count,
        narrow=narrow_count,
        inputs=samples.shape[0],
        per_device=per_device,
        points=points,
        taps=tap_count,
        pols=pols,
        dishes=dishes,
        beams=beams,
        spectra=frames - tap_count + 1,
        extent=smooth_kernel.shape[0],
    )

    def owner_of(column):
        device_slot = column // per_device
        return (
            device_slot % narrow_count * wide_count + device_slot // narrow_count
        ) * per_device + column % per_device

    table = jnp.asarray(fourier_rows(points, owner_of, wide_count))
    filtered = fused(samples, filter_taps, table, beam_weights, smooth_kernel, plan)
    return filtered.reshape(plan.local, plan.all_bins, plan.share)


def solution(mesh):
    placed = (
        P(("wide", "narrow"), None, None),
        P(),
        P(("narrow", "wide"), None, None, None, None),
        P(),
    )
    return jax.shard_map(
        body, mesh=mesh, in_specs=placed, out_specs=P("narrow", None, "wide"), check_vma=False
    )
```

```python
import dataclasses
import functools

import jax
import jax.numpy as jnp
import numpy as np
from jax import lax
from jax.experimental import pallas as pl
from jax.experimental.pallas import tpu as pltpu
from jax.sharding import PartitionSpec as P

INTEG = 8
LANES = 128
BAND = 8
SLOTS = 3
LAG = 2
PAIRS = 2
HALO_LAG = 4
SMOOTH_LAG = 5
MESH = pl.DeviceIdType.MESH


@dataclasses.dataclass(frozen=True)
class Plan:
    wide: int
    narrow: int
    inputs: int
    per_device: int
    points: int
    taps: int
    pols: int
    dishes: int
    beams: int
    spectra: int
    extent: int

    @property
    def devices(self):
        return self.wide * self.narrow

    @property
    def groups(self):
        return max(1, self.inputs // 16)

    @property
    def rows(self):
        return self.inputs // self.groups

    @property
    def span(self):
        return LANES // (2 * self.groups)

    @property
    def chunks(self):
        return self.spectra // self.span

    @property
    def bins(self):
        return self.span // INTEG

    @property
    def turns(self):
        return self.rows // (2 * PAIRS)

    @property
    def together(self):
        return 8 // self.bins

    @property
    def sets(self):
        return self.per_device // self.together

    @property
    def halves(self):
        return self.points // LANES

    @property
    def tiles(self):
        return (self.span + self.taps - 1) * self.halves

    @property
    def per_pol(self):
        return self.devices // self.pols

    @property
    def half(self):
        return self.extent // 2

    @property
    def share(self):
        return self.beams // self.wide

    @property
    def local(self):
        return self.wide * self.per_device

    @property
    def all_bins(self):
        return self.spectra // INTEG

    @property
    def reach(self):
        return (BAND + self.extent - 1) * self.bins

    @property
    def lanes(self):
        return -(-self.reach // LANES) * LANES

    @property
    def shifts(self):
        return -(-(2 * self.all_bins - self.bins) // 8) * 8


def fourier_rows(points, owner_of, blocks):
    column = np.arange(points)
    phase_index = owner_of(column)[:, None] * column[None, :] % points
    angles = phase_index * (2.0 * np.pi / points)
    cosine = np.cos(angles) / np.sqrt(points)
    sine_part = np.sin(angles) / np.sqrt(points)
    real_row = np.concatenate([cosine, sine_part], axis=1)
    imag_row = np.concatenate([-sine_part, cosine], axis=1)
    table = np.stack([part.reshape(blocks, -1, 2 * points) for part in (real_row, imag_row)], axis=1)
    table = table.reshape(2 * points, 2 * points).astype(np.float32)
    high = table.astype(jnp.bfloat16)
    return np.stack([high, (table - high.astype(np.float32)).astype(jnp.bfloat16)])


def one_hot(shape, matches):
    row = lax.broadcasted_iota(jnp.int32, shape, 0)
    column = lax.broadcasted_iota(jnp.int32, shape, 1)
    return matches(row, column).astype(jnp.float32)


def exact_dot(left, right, contract=(1, 0)):
    return lax.dot_general(
        left,
        right,
        (((contract[0],), (contract[1],)), ((), ())),
        precision=lax.Precision.HIGHEST,
        preferred_element_type=jnp.float32,
    )


def split(value):
    high = value.astype(jnp.bfloat16)
    return high, (value - high.astype(jnp.float32)).astype(jnp.bfloat16)


def fused_kernel(
    plan,
    taps_ref,
    smooth_ref,
    table_hbm,
    samples_ref,
    weights_ref,
    recv_ref,
    out_ref,
    table_ref,
    raw_ref,
    window_ref,
    signal_ref,
    stage_ref,
    send_ref,
    weight_ref,
    land_ref,
    energy_ref,
    shifted_ref,
    matrix_ref,
    outgoing_ref,
    gather_ref,
    raw_sem,
    table_sem,
    weight_sem,
    send_sem,
    recv_sem,
    last_sem,
    land_sem,
    share_sem,
    gather_sem,
    up_sem,
    down_sem,
    low_sem,
    high_sem,
):
    span, rows, groups, halves = plan.span, plan.rows, plan.groups, plan.halves
    tap_count, points, chunks = plan.taps, plan.points, plan.chunks
    my_wide = lax.axis_index("wide")
    my_narrow = lax.axis_index("narrow")
    me = my_wide * plan.narrow + my_narrow

    def peer(step):
        return (
            lax.rem(my_wide + step // plan.narrow, plan.wide),
            lax.rem(my_narrow + step % plan.narrow, plan.narrow),
        )

    def load_raw(chunk, slot):
        @pl.loop(0, plan.tiles)
        def _(tile):
            column = pl.multiple_of((chunk * span * halves + tile) * LANES, LANES)
            pltpu.make_async_copy(
                samples_ref.at[:, :, pl.ds(column, LANES)], raw_ref.at[slot, tile], raw_sem.at[slot]
            ).start()

    last = chunks - 1
    own_start = plan.half * plan.bins
    own_rows = plan.local * plan.bins
    part_rows = plan.per_device * plan.bins

    barrier = pltpu.get_barrier_semaphore()

    @pl.loop(1, plan.devices)
    def _(step):
        pl.semaphore_signal(barrier, inc=1, device_id=peer(step), device_id_type=MESH)

    load_raw(0, 0)
    pltpu.make_async_copy(table_hbm, table_ref, table_sem).start()

    @pl.loop(0, plan.per_device)
    def _(channel):
        pltpu.make_async_copy(
            weights_ref.at[channel], weight_ref.at[channel], weight_sem
        ).start()

    out_ref[...] = jnp.zeros_like(out_ref)

    def clear(start):
        gather_ref[:, start : start + own_start] = jnp.zeros(
            (chunks, own_start, plan.share), jnp.bfloat16
        )

    @pl.when(my_narrow == 0)
    def _():
        clear(0)

    @pl.when(my_narrow == plan.narrow - 1)
    def _():
        clear(own_start + own_rows)

    def filter_rows(slot):
        row_groups = 2 * plan.inputs // 8

        @pl.loop(0, halves * row_groups)
        def _(index):
            half = index // row_groups
            group = index % row_groups
            columns = pl.ds(pl.multiple_of(half * LANES, LANES), LANES)
            coeffs = [
                jnp.broadcast_to(taps_ref[tap : tap + 1, columns], (8, LANES))
                for tap in range(tap_count)
            ]
            sums = {}
            for frame in range(span + tap_count - 1):
                piece = raw_ref[slot, frame * halves + half, pl.ds(group * 4, 4)]
                value = piece.reshape(8, LANES).astype(jnp.float32)
                for out in range(max(0, frame - tap_count + 1), min(span - 1, frame) + 1):
                    term = coeffs[frame - out] * value
                    sums[out] = sums[out] + term if out in sums else term
                done = frame - tap_count + 1
                if done >= 0:
                    base = group * (8 * span) + done
                    window_ref[half, pl.ds(base, 8, stride=span), :] = sums.pop(done)

    def prepare():
        @pl.loop(0, plan.turns)
        def _(step):
            pieces = []
            for pair in range(PAIRS):
                for group in range(groups):
                    for member in range(2):
                        source = group * rows + step * (2 * PAIRS) + 2 * pair + member
                        blocks = []
                        for part in range(2):
                            start = pl.multiple_of((2 * source + part) * span, span)
                            for half in range(halves):
                                blocks.append(window_ref[half, pl.ds(start, span), :])
                        pieces.append(jnp.concatenate(blocks, axis=1))
            signal_ref[0, step], signal_ref[1, step] = split(jnp.concatenate(pieces, axis=0))

    def transform(block, slot):
        channels = plan.narrow * plan.per_device
        lane = lax.broadcasted_iota(jnp.int32, (channels, LANES), 1)
        first = lane % (2 * span) < span
        product = functools.partial(
            lax.dot_general,
            dimension_numbers=(((1,), (1,)), ((), ())),
            preferred_element_type=jnp.float32,
        )
        table_rows = pl.ds(pl.multiple_of(block * (2 * channels), 2 * channels), 2 * channels)

        @pl.loop(0, plan.turns)
        def _(step):
            high, low = signal_ref[0, step], signal_ref[1, step]
            result = (
                product(table_ref[1, table_rows], high)
                + product(table_ref[0, table_rows], low)
                + product(table_ref[0, table_rows], high)
            )
            for pair in range(PAIRS):
                real = result[:channels, pair * LANES : (pair + 1) * LANES]
                imag = result[channels:, pair * LANES : (pair + 1) * LANES]
                row = step * (2 * PAIRS) + 2 * pair
                stage_ref[pl.ds(row, channels, stride=rows), :] = jnp.where(
                    first, real, pltpu.roll(imag, span, 1)
                )
                stage_ref[pl.ds(row + 1, channels, stride=rows), :] = jnp.where(
                    first, pltpu.roll(real, LANES - span, 1), imag
                )

        place = pl.ds(pl.multiple_of(block * channels, channels), channels)
        send_ref[slot, place] = (
            stage_ref[...].reshape(channels, rows, LANES).astype(jnp.bfloat16)
        )

    def block_at(step):
        moved = lax.rem(step + plan.wide // 2, plan.wide)
        if plan.wide & (plan.wide - 1) == 0:
            return lax.bitwise_xor(my_wide, moved)
        return lax.rem(my_wide + moved, plan.wide)

    def start_sends(chunk, block, slot):
        @pl.loop(0, plan.narrow)
        def _(step):
            narrow = lax.rem(my_narrow + step, plan.narrow)
            target = block * plan.narrow + narrow
            source = send_ref.at[slot, pl.ds(target * plan.per_device, plan.per_device)]

            @pl.when(target != me)
            def _():
                pltpu.make_async_remote_copy(
                    src_ref=source,
                    dst_ref=recv_ref.at[chunk, me],
                    send_sem=send_sem.at[slot],
                    recv_sem=recv_sem.at[chunk],
                    device_id=(block, narrow),
                    device_id_type=MESH,
                ).start()

            @pl.when(target == me)
            def _():
                pltpu.make_async_copy(source, recv_ref.at[chunk, me], recv_sem.at[chunk]).start()

    def start_last(index, slot):
        def voltages(target):
            first = target * plan.per_device + index * plan.together
            return send_ref.at[slot, pl.ds(first, plan.together)]

        landing = land_ref.at[1, me, pl.ds(index * plan.together, plan.together)]

        @pl.loop(1, plan.devices)
        def _(step):
            wide, narrow = peer(step)
            pltpu.make_async_remote_copy(
                src_ref=voltages(wide * plan.narrow + narrow),
                dst_ref=landing,
                send_sem=send_sem.at[slot],
                recv_sem=last_sem.at[index],
                device_id=(wide, narrow),
                device_id_type=MESH,
            ).start()

        pltpu.make_async_copy(voltages(me), landing, last_sem.at[index]).start()

    def wait_sends(slot):
        sent = send_ref.at[slot, pl.ds(0, (plan.devices - 1) * plan.per_device)]
        pltpu.make_async_copy(sent, sent, send_sem.at[slot]).wait()

    def form_beams(chunk):
        together = plan.together
        landed = (chunk == last).astype(jnp.int32)

        @pl.when(chunk < last)
        def _():
            arrived = recv_ref.at[chunk]
            pltpu.make_async_copy(arrived, arrived, recv_sem.at[chunk]).wait()
            landing = pltpu.make_async_copy(arrived, land_ref.at[0], land_sem)
            landing.start()
            landing.wait()

        @pl.loop(0, plan.sets)
        def _(step):
            if plan.sets > 2:

                @pl.when((chunk == last - 1) & (step == 0))
                def _():
                    start_last(plan.sets - 2, last % SLOTS)

            if plan.sets > 1:

                @pl.when((chunk == last - 1) & (step == plan.sets - 1))
                def _():
                    start_last(plan.sets - 1, last % SLOTS)

            @pl.when((chunk == last) & (step == plan.sets - 1))
            def _():
                catch_up()

            @pl.when(chunk == last)
            def _():
                arrived = land_ref.at[1, :, pl.ds(step * together, together)]
                pltpu.make_async_copy(arrived, arrived, last_sem.at[step]).wait()

            binned = []
            for member in range(together):
                channel = step * together + member
                energy = None
                for pol in range(plan.pols):
                    block = land_ref[landed, pol * plan.per_pol : (pol + 1) * plan.per_pol, channel]
                    block = block.astype(jnp.float32).reshape(plan.per_pol * rows, LANES)
                    turned = block.T.astype(jnp.bfloat16)
                    formed = None
                    for group in range(groups):
                        base = 2 * span * group
                        straight = turned[base : base + 2 * span]
                        crossed = jnp.concatenate(
                            [-straight[span:], straight[:span]], axis=0
                        )
                        for side, left in enumerate((straight, crossed)):
                            right = weight_ref[channel, pol, side, :, group]
                            right = right.reshape(-1, plan.beams)
                            term = jnp.dot(left, right, preferred_element_type=jnp.float32)
                            formed = term if formed is None else formed + term
                    squares = formed * formed
                    power = squares[:span] + squares[span:]
                    energy = power if energy is None else energy + power
                binned.append(energy.reshape(plan.bins, INTEG, plan.beams).sum(axis=1))
            energy_ref[pl.ds(pl.multiple_of(step * 8, 8), 8), :] = jnp.concatenate(
                binned, axis=0
            )

        scale = jnp.float32(1.0 / (plan.pols * INTEG))
        intensity = (energy_ref[...] * scale).astype(jnp.bfloat16)
        for owner in range(plan.wide):
            outgoing_ref[chunk, owner] = intensity[:, owner * plan.share : (owner + 1) * plan.share]

        mine = pl.ds(pl.multiple_of(own_start + my_wide * part_rows, part_rows), part_rows)

        @pl.loop(1, plan.wide)
        def _(step):
            target = lax.rem(my_wide + step, plan.wide)
            pltpu.make_async_remote_copy(
                src_ref=outgoing_ref.at[chunk, target],
                dst_ref=gather_ref.at[chunk, mine],
                send_sem=share_sem.at[chunk],
                recv_sem=gather_sem.at[chunk],
                device_id=(target, my_narrow),
                device_id_type=MESH,
            ).start()

        pltpu.make_async_copy(
            outgoing_ref.at[chunk, my_wide], gather_ref.at[chunk, mine], gather_sem.at[chunk]
        ).start()

    def halo(chunk):
        def upward():
            return pltpu.make_async_remote_copy(
                src_ref=gather_ref.at[chunk, pl.ds(own_rows, own_start)],
                dst_ref=gather_ref.at[chunk, pl.ds(0, own_start)],
                send_sem=up_sem.at[chunk],
                recv_sem=low_sem.at[chunk],
                device_id=(my_wide, my_narrow + 1),
                device_id_type=MESH,
            )

        def downward():
            return pltpu.make_async_remote_copy(
                src_ref=gather_ref.at[chunk, pl.ds(own_start, own_start)],
                dst_ref=gather_ref.at[chunk, pl.ds(own_start + own_rows, own_start)],
                send_sem=down_sem.at[chunk],
                recv_sem=high_sem.at[chunk],
                device_id=(my_wide, my_narrow - 1),
                device_id_type=MESH,
            )

        return upward, downward

    def start_halo(chunk):
        own = gather_ref.at[chunk, pl.ds(own_start, own_rows)]
        pltpu.make_async_copy(own, own, gather_sem.at[chunk]).wait()
        upward, downward = halo(chunk)

        @pl.when(my_narrow < plan.narrow - 1)
        def _():
            upward().start()

        @pl.when(my_narrow > 0)
        def _():
            downward().start()

    def build_matrix():
        extent, bins, shifts, lanes = plan.extent, plan.bins, plan.shifts, plan.lanes
        last = plan.all_bins - bins
        spread = one_hot((extent, lanes), lambda row, column: row == column // bins)
        columns = exact_dot(smooth_ref[...], spread, (0, 0))
        inner = lax.broadcasted_iota(jnp.int32, (shifts, lanes), 1) % bins
        shifted = jnp.zeros((shifts, lanes), jnp.float32)
        for offset in range(bins):
            select = one_hot(
                (shifts, extent),
                lambda row, column: column == offset - row + last + plan.half,
            )
            shifted = jnp.where(inner == offset, exact_dot(select, columns), shifted)
        shifted_ref[...] = shifted
        gather = one_hot(
            (plan.all_bins, shifts),
            lambda row, column: (column >= row)
            & (column <= row + last)
            & ((column - row) % bins == 0),
        )
        block = one_hot((lanes, lanes), lambda row, column: row // bins == column // bins)
        total = exact_dot(exact_dot(gather, shifted), block)
        mean = total * jnp.float32(1.0 / plan.all_bins)

        @pl.loop(0, chunks)
        def _(chunk):
            start = shifts - (last - bins * chunk)
            rows_here = pltpu.roll(shifted_ref[...], lax.rem(start, shifts), 0)[: plan.all_bins]
            centered = rows_here - mean
            for channel in range(BAND):
                moved = pltpu.roll(centered, bins * channel, 1) if channel else centered
                place = slice(channel * plan.all_bins, (channel + 1) * plan.all_bins)
                matrix_ref[chunk, 0, place], matrix_ref[chunk, 1, place] = split(moved)

    def smooth(chunk):
        upward, downward = halo(chunk)

        @pl.when(my_narrow > 0)
        def _():
            upward().wait_recv()

        @pl.when(my_narrow < plan.narrow - 1)
        def _():
            downward().wait_recv()

        for band in range(plan.local // BAND):
            start = band * BAND * plan.bins
            values = gather_ref[chunk, start : start + plan.reach]
            size = BAND * plan.all_bins
            place = slice(band * size, (band + 1) * size)
            total = out_ref[place]
            for side in (1, 0):
                total = total + jnp.dot(
                    matrix_ref[chunk, side, :, : plan.reach],
                    values,
                    preferred_element_type=jnp.float32,
                )
            out_ref[place] = total

    def catch_up():
        start_halo(last - 2)
        smooth(last - 3)
        smooth(last - 2)

    @pl.loop(0, chunks + LAG)
    def _(step):
        @pl.when(step < chunks)
        def _():
            side = step % 2
            slot = step % SLOTS
            raw = raw_ref.at[side]
            pltpu.make_async_copy(raw, raw, raw_sem.at[side]).wait()

            @pl.when(step + 1 < chunks)
            def _():
                load_raw(step + 1, 1 - side)

            filter_rows(side)

            @pl.when(step >= SLOTS)
            def _():
                wait_sends(slot)

            @pl.when(step == 0)
            def _():
                pltpu.make_async_copy(table_hbm, table_ref, table_sem).wait()

            prepare()

            @pl.loop(0, plan.wide)
            def _(turn):
                block = block_at(turn)
                transform(block, slot)

                @pl.when((step == 0) & (turn == 0))
                def _():
                    pl.semaphore_wait(barrier, plan.devices - 1)

                @pl.when(step < last)
                def _():
                    start_sends(step, block, slot)

            @pl.when(step == last)
            def _():
                @pl.loop(0, max(1, plan.sets - 2))
                def _(index):
                    start_last(index, slot)

        @pl.when(step == LAG)
        def _():
            build_matrix()
            pltpu.make_async_copy(weight_ref, weight_ref, weight_sem).wait()

        @pl.when(step >= LAG)
        def _():
            form_beams(step - LAG)

        @pl.when((step >= HALO_LAG) & (step <= last + 1))
        def _():
            start_halo(step - HALO_LAG)

        @pl.when((step >= SMOOTH_LAG) & (step <= last + 1))
        def _():
            smooth(step - SMOOTH_LAG)

    start_halo(last - 1)
    smooth(last - 1)
    start_halo(last)
    smooth(last)

    for slot in range(min(SLOTS, chunks)):
        wait_sends(slot)

    @pl.loop(0, chunks)
    def _(chunk):
        sent = outgoing_ref.at[chunk, pl.ds(0, plan.wide - 1)]
        pltpu.make_async_copy(sent, sent, share_sem.at[chunk]).wait()
        upward, downward = halo(chunk)

        @pl.when(my_narrow < plan.narrow - 1)
        def _():
            upward().wait_send()

        @pl.when(my_narrow > 0)
        def _():
            downward().wait_send()


def fused(samples, filter_taps, table, beam_weights, smooth_kernel, plan):
    if plan.groups == 1:
        dish_split = (1, 1, plan.dishes)
    else:
        dish_split = (plan.per_pol, plan.groups, plan.rows)
    weight_shape = (plan.per_device, plan.pols, 2, *dish_split, plan.beams)
    weights = beam_weights.reshape(weight_shape)
    anywhere = pl.BlockSpec(memory_space=pl.ANY)
    local = pl.BlockSpec(memory_space=pltpu.VMEM)
    recv_shape = (plan.chunks - 1, plan.devices, plan.per_device, plan.rows, LANES)
    energy_shape = (plan.per_device * plan.bins, plan.beams)
    ext_rows = (plan.local + 2 * plan.half) * plan.bins
    out_shape = (plan.local * plan.all_bins, plan.share)
    per_chunk = pltpu.SemaphoreType.DMA((plan.chunks,))
    return pl.pallas_call(
        functools.partial(fused_kernel, plan),
        in_specs=[local, local, anywhere, anywhere, anywhere],
        out_specs=[anywhere, local],
        out_shape=[
            jax.ShapeDtypeStruct(recv_shape, jnp.bfloat16),
            pltpu.VMEM(out_shape, jnp.float32),
        ],
        scratch_shapes=[
            pltpu.VMEM(table.shape, jnp.bfloat16),
            pltpu.VMEM((2, plan.tiles, plan.inputs, 2, LANES), jnp.bfloat16),
            pltpu.VMEM((plan.halves, 2 * plan.inputs * plan.span, LANES), jnp.float32),
            pltpu.VMEM((2, plan.turns, 2 * PAIRS * plan.groups * plan.span, 2 * plan.points), jnp.bfloat16),
            pltpu.VMEM((plan.points // plan.wide * plan.rows, LANES), jnp.float32),
            pltpu.VMEM((SLOTS, plan.points, plan.rows, LANES), jnp.bfloat16),
            pltpu.VMEM(weight_shape, jnp.bfloat16),
            pltpu.VMEM((2, *recv_shape[1:]), jnp.bfloat16),
            pltpu.VMEM(energy_shape, jnp.float32),
            pltpu.VMEM((plan.shifts, plan.lanes), jnp.float32),
            pltpu.VMEM((plan.chunks, 2, BAND * plan.all_bins, plan.lanes), jnp.bfloat16),
            pltpu.VMEM(
                (plan.chunks, plan.wide, plan.per_device * plan.bins, plan.share), jnp.bfloat16
            ),
            pltpu.VMEM((plan.chunks, ext_rows, plan.share), jnp.bfloat16),
            pltpu.SemaphoreType.DMA((2,)),
            pltpu.SemaphoreType.DMA,
            pltpu.SemaphoreType.DMA,
            pltpu.SemaphoreType.DMA((SLOTS,)),
            per_chunk,
            pltpu.SemaphoreType.DMA((plan.sets,)),
            pltpu.SemaphoreType.DMA,
            *([per_chunk] * 6),
        ],
        compiler_params=pltpu.CompilerParams(
            collective_id=0, has_side_effects=True, vmem_limit_bytes=62 * 1000 * 1000
        ),
        name="fused",
    )(filter_taps, smooth_kernel, table, samples, weights)[1]


def body(samples, filter_taps, beam_weights, smooth_kernel):
    tap_count, points = filter_taps.shape
    wide_count = lax.axis_size("wide")
    narrow_count = lax.axis_size("narrow")
    per_device, pols, _, dishes, beams = beam_weights.shape
    frames = samples.shape[2] // points
    plan = Plan(
        wide=wide_count,
        narrow=narrow_count,
        inputs=samples.shape[0],
        per_device=per_device,
        points=points,
        taps=tap_count,
        pols=pols,
        dishes=dishes,
        beams=beams,
        spectra=frames - tap_count + 1,
        extent=smooth_kernel.shape[0],
    )

    def owner_of(column):
        device_slot = column // per_device
        return (
            device_slot % narrow_count * wide_count + device_slot // narrow_count
        ) * per_device + column % per_device

    table = jnp.asarray(fourier_rows(points, owner_of, wide_count))
    filtered = fused(samples, filter_taps, table, beam_weights, smooth_kernel, plan)
    return filtered.reshape(plan.local, plan.all_bins, plan.share)


def solution(mesh):
    placed = (
        P(("wide", "narrow"), None, None),
        P(),
        P(("narrow", "wide"), None, None, None, None),
        P(),
    )
    return jax.shard_map(
        body, mesh=mesh, in_specs=placed, out_specs=P("narrow", None, "wide"), check_vma=False
    )
```

```python
import dataclasses
import functools

import jax
import jax.numpy as jnp
import numpy as np
from jax import lax
from jax.experimental import pallas as pl
from jax.experimental.pallas import tpu as pltpu
from jax.sharding import PartitionSpec as P

INTEG = 8
LANES = 128
BAND = 8
SLOTS = 4
LAG = 2
PAIRS = 2
HELD = 1
HALO_LAG = 4
SMOOTH_LAG = 5
MESH = pl.DeviceIdType.MESH


@dataclasses.dataclass(frozen=True)
class Plan:
    wide: int
    narrow: int
    inputs: int
    per_device: int
    points: int
    taps: int
    pols: int
    dishes: int
    beams: int
    spectra: int
    extent: int

    @property
    def devices(self):
        return self.wide * self.narrow

    @property
    def groups(self):
        return max(1, self.inputs // 16)

    @property
    def rows(self):
        return self.inputs // self.groups

    @property
    def span(self):
        return LANES // (2 * self.groups)

    @property
    def chunks(self):
        return self.spectra // self.span

    @property
    def bins(self):
        return self.span // INTEG

    @property
    def turns(self):
        return self.rows // (2 * PAIRS)

    @property
    def together(self):
        return 8 // self.bins

    @property
    def sets(self):
        return self.per_device // self.together

    @property
    def halves(self):
        return self.points // LANES

    @property
    def tiles(self):
        return (self.span + self.taps - 1) * self.halves

    @property
    def per_pol(self):
        return self.devices // self.pols

    @property
    def half(self):
        return self.extent // 2

    @property
    def share(self):
        return self.beams // self.wide

    @property
    def local(self):
        return self.wide * self.per_device

    @property
    def all_bins(self):
        return self.spectra // INTEG

    @property
    def reach(self):
        return (BAND + self.extent - 1) * self.bins

    @property
    def lanes(self):
        return -(-self.reach // LANES) * LANES

    @property
    def shifts(self):
        return -(-(2 * self.all_bins - self.bins) // 8) * 8


def fourier_rows(points, owner_of, blocks):
    column = np.arange(points)
    phase_index = owner_of(column)[:, None] * column[None, :] % points
    angles = phase_index * (2.0 * np.pi / points)
    cosine = np.cos(angles) / np.sqrt(points)
    sine_part = np.sin(angles) / np.sqrt(points)
    real_row = np.concatenate([cosine, sine_part], axis=1)
    imag_row = np.concatenate([-sine_part, cosine], axis=1)
    table = np.stack([part.reshape(blocks, -1, 2 * points) for part in (real_row, imag_row)], axis=1)
    table = table.reshape(2 * points, 2 * points).astype(np.float32)
    high = table.astype(jnp.bfloat16)
    return np.stack([high, (table - high.astype(np.float32)).astype(jnp.bfloat16)])


def one_hot(shape, matches):
    row = lax.broadcasted_iota(jnp.int32, shape, 0)
    column = lax.broadcasted_iota(jnp.int32, shape, 1)
    return matches(row, column).astype(jnp.float32)


def exact_dot(left, right, contract=(1, 0)):
    return lax.dot_general(
        left,
        right,
        (((contract[0],), (contract[1],)), ((), ())),
        precision=lax.Precision.HIGHEST,
        preferred_element_type=jnp.float32,
    )


def split(value):
    high = value.astype(jnp.bfloat16)
    return high, (value - high.astype(jnp.float32)).astype(jnp.bfloat16)


def fused_kernel(
    plan,
    taps_ref,
    smooth_ref,
    table_hbm,
    samples_ref,
    weights_ref,
    recv_ref,
    out_ref,
    table_ref,
    raw_ref,
    window_ref,
    signal_ref,
    stage_ref,
    send_ref,
    weight_ref,
    land_ref,
    energy_ref,
    shifted_ref,
    matrix_ref,
    outgoing_ref,
    gather_ref,
    raw_sem,
    table_sem,
    weight_sem,
    send_sem,
    recv_sem,
    last_sem,
    land_sem,
    share_sem,
    gather_sem,
    up_sem,
    down_sem,
    low_sem,
    high_sem,
):
    span, rows, groups, halves = plan.span, plan.rows, plan.groups, plan.halves
    tap_count, points, chunks = plan.taps, plan.points, plan.chunks
    my_wide = lax.axis_index("wide")
    my_narrow = lax.axis_index("narrow")
    me = my_wide * plan.narrow + my_narrow

    def peer(step):
        return (
            lax.rem(my_wide + step // plan.narrow, plan.wide),
            lax.rem(my_narrow + step % plan.narrow, plan.narrow),
        )

    def load_raw(chunk, slot):
        @pl.loop(0, plan.tiles)
        def _(tile):
            column = pl.multiple_of((chunk * span * halves + tile) * LANES, LANES)
            pltpu.make_async_copy(
                samples_ref.at[:, :, pl.ds(column, LANES)], raw_ref.at[slot, tile], raw_sem.at[slot]
            ).start()

    last = chunks - 1
    own_start = plan.half * plan.bins
    own_rows = plan.local * plan.bins
    part_rows = plan.per_device * plan.bins

    barrier = pltpu.get_barrier_semaphore()
    load_raw(0, 0)
    pltpu.make_async_copy(table_hbm, table_ref, table_sem).start()

    @pl.loop(1, plan.devices)
    def _(step):
        pl.semaphore_signal(barrier, inc=1, device_id=peer(step), device_id_type=MESH)

    @pl.loop(0, plan.per_device)
    def _(channel):
        pltpu.make_async_copy(
            weights_ref.at[channel], weight_ref.at[channel], weight_sem
        ).start()

    out_ref[...] = jnp.zeros_like(out_ref)

    def clear(start):
        gather_ref[:, start : start + own_start] = jnp.zeros(
            (chunks, own_start, plan.share), jnp.bfloat16
        )

    @pl.when(my_narrow == 0)
    def _():
        clear(0)

    @pl.when(my_narrow == plan.narrow - 1)
    def _():
        clear(own_start + own_rows)

    def filter_rows(slot):
        row_groups = 2 * plan.inputs // 8

        @pl.loop(0, halves * row_groups)
        def _(index):
            half = index // row_groups
            group = index % row_groups
            columns = pl.ds(pl.multiple_of(half * LANES, LANES), LANES)
            coeffs = [
                jnp.broadcast_to(taps_ref[tap : tap + 1, columns], (8, LANES))
                for tap in range(tap_count)
            ]
            sums = {}
            for frame in range(span + tap_count - 1):
                view = raw_ref.at[slot, frame * halves + half].reshape(2 * plan.inputs, LANES)
                value = view[pl.ds(pl.multiple_of(group * 8, 8), 8)].astype(jnp.float32)
                for out in range(max(0, frame - tap_count + 1), min(span - 1, frame) + 1):
                    term = coeffs[frame - out] * value
                    sums[out] = sums[out] + term if out in sums else term
                done = frame - tap_count + 1
                if done >= 0:
                    base = group * (8 * span) + done
                    window_ref[half, pl.ds(base, 8, stride=span), :] = sums.pop(done)

    def prepare():
        @pl.loop(0, plan.turns)
        def _(step):
            pieces = []
            for pair in range(PAIRS):
                for group in range(groups):
                    for member in range(2):
                        source = group * rows + step * (2 * PAIRS) + 2 * pair + member
                        blocks = []
                        for part in range(2):
                            start = pl.multiple_of((2 * source + part) * span, span)
                            for half in range(halves):
                                blocks.append(window_ref[half, pl.ds(start, span), :])
                        pieces.append(jnp.concatenate(blocks, axis=1))
            signal_ref[0, step], signal_ref[1, step] = split(jnp.concatenate(pieces, axis=0))

    def transform(block, slot):
        channels = plan.narrow * plan.per_device
        lane = lax.broadcasted_iota(jnp.int32, (channels, LANES), 1)
        first = lane % (2 * span) < span
        product = functools.partial(
            lax.dot_general,
            dimension_numbers=(((1,), (1,)), ((), ())),
            preferred_element_type=jnp.float32,
        )
        table_rows = pl.ds(pl.multiple_of(block * (2 * channels), 2 * channels), 2 * channels)

        @pl.loop(0, plan.turns)
        def _(step):
            high, low = signal_ref[0, step], signal_ref[1, step]
            result = (
                product(table_ref[1, table_rows], high)
                + product(table_ref[0, table_rows], low)
                + product(table_ref[0, table_rows], high)
            )
            for pair in range(PAIRS):
                real = result[:channels, pair * LANES : (pair + 1) * LANES]
                imag = result[channels:, pair * LANES : (pair + 1) * LANES]
                row = step * (2 * PAIRS) + 2 * pair
                stage_ref[pl.ds(row, channels, stride=rows), :] = jnp.where(
                    first, real, pltpu.roll(imag, span, 1)
                )
                stage_ref[pl.ds(row + 1, channels, stride=rows), :] = jnp.where(
                    first, pltpu.roll(real, LANES - span, 1), imag
                )

        place = pl.ds(pl.multiple_of(block * channels, channels), channels)
        send_ref[slot, place] = (
            stage_ref[...].reshape(channels, rows, LANES).astype(jnp.bfloat16)
        )

    def block_at(step):
        moved = lax.rem(step + plan.wide // 2, plan.wide)
        if plan.wide & (plan.wide - 1) == 0:
            return lax.bitwise_xor(my_wide, moved)
        return lax.rem(my_wide + moved, plan.wide)

    def start_sends(chunk, block, slot):
        @pl.loop(0, plan.narrow)
        def _(step):
            narrow = lax.rem(my_narrow + step, plan.narrow)
            target = block * plan.narrow + narrow
            source = send_ref.at[slot, pl.ds(target * plan.per_device, plan.per_device)]

            @pl.when(target != me)
            def _():
                pltpu.make_async_remote_copy(
                    src_ref=source,
                    dst_ref=recv_ref.at[chunk, me],
                    send_sem=send_sem.at[slot],
                    recv_sem=recv_sem.at[chunk],
                    device_id=(block, narrow),
                    device_id_type=MESH,
                ).start()

            @pl.when(target == me)
            def _():
                pltpu.make_async_copy(source, recv_ref.at[chunk, me], recv_sem.at[chunk]).start()

    def start_last(index, slot):
        def voltages(target):
            first = target * plan.per_device + index * plan.together
            return send_ref.at[slot, pl.ds(first, plan.together)]

        landing = land_ref.at[1, me, pl.ds(index * plan.together, plan.together)]

        @pl.loop(1, plan.devices)
        def _(step):
            wide, narrow = peer(step)
            pltpu.make_async_remote_copy(
                src_ref=voltages(wide * plan.narrow + narrow),
                dst_ref=landing,
                send_sem=send_sem.at[slot],
                recv_sem=last_sem.at[index],
                device_id=(wide, narrow),
                device_id_type=MESH,
            ).start()

        pltpu.make_async_copy(voltages(me), landing, last_sem.at[index]).start()

    def wait_sends(slot):
        sent = send_ref.at[slot, pl.ds(0, (plan.devices - 1) * plan.per_device)]
        pltpu.make_async_copy(sent, sent, send_sem.at[slot]).wait()

    def share_intensity(chunk):
        mine = pl.ds(pl.multiple_of(own_start + my_wide * part_rows, part_rows), part_rows)

        @pl.loop(1, plan.wide)
        def _(step):
            target = lax.rem(my_wide + step, plan.wide)
            pltpu.make_async_remote_copy(
                src_ref=outgoing_ref.at[chunk, target],
                dst_ref=gather_ref.at[chunk, mine],
                send_sem=share_sem.at[chunk],
                recv_sem=gather_sem.at[chunk],
                device_id=(target, my_narrow),
                device_id_type=MESH,
            ).start()

        pltpu.make_async_copy(
            outgoing_ref.at[chunk, my_wide], gather_ref.at[chunk, mine], gather_sem.at[chunk]
        ).start()

    def form_beams(chunk):
        together = plan.together
        landed = (chunk == last).astype(jnp.int32)

        @pl.when(chunk < last)
        def _():
            arrived = recv_ref.at[chunk]
            pltpu.make_async_copy(arrived, arrived, recv_sem.at[chunk]).wait()
            landing = pltpu.make_async_copy(arrived, land_ref.at[0], land_sem)
            landing.start()
            landing.wait()

        @pl.loop(0, plan.sets)
        def _(step):
            @pl.when((chunk == last) & (step == plan.sets - 1))
            def _():
                catch_up()

            @pl.when(chunk == last)
            def _():
                arrived = land_ref.at[1, :, pl.ds(step * together, together)]
                pltpu.make_async_copy(arrived, arrived, last_sem.at[step]).wait()

            @pl.when((chunk == last) & (step == plan.sets - 1))
            def _():
                for held in range(HELD, 0, -1):
                    share_intensity(last - held)

            binned = []
            for member in range(together):
                channel = step * together + member
                energy = None
                for pol in range(plan.pols):
                    block = land_ref[landed, pol * plan.per_pol : (pol + 1) * plan.per_pol, channel]
                    block = block.astype(jnp.float32).reshape(plan.per_pol * rows, LANES)
                    turned = block.T.astype(jnp.bfloat16)
                    formed = None
                    for group in range(groups):
                        base = 2 * span * group
                        straight = turned[base : base + 2 * span]
                        crossed = jnp.concatenate(
                            [-straight[span:], straight[:span]], axis=0
                        )
                        for side, left in enumerate((straight, crossed)):
                            right = weight_ref[channel, pol, side, :, group]
                            right = right.reshape(-1, plan.beams)
                            term = jnp.dot(left, right, preferred_element_type=jnp.float32)
                            formed = term if formed is None else formed + term
                    squares = formed * formed
                    power = squares[:span] + squares[span:]
                    energy = power if energy is None else energy + power
                binned.append(energy.reshape(plan.bins, INTEG, plan.beams).sum(axis=1))
            energy_ref[pl.ds(pl.multiple_of(step * 8, 8), 8), :] = jnp.concatenate(
                binned, axis=0
            )

        scale = jnp.float32(1.0 / (plan.pols * INTEG))
        intensity = (energy_ref[...] * scale).astype(jnp.bfloat16)
        for owner in range(plan.wide):
            outgoing_ref[chunk, owner] = intensity[:, owner * plan.share : (owner + 1) * plan.share]

        @pl.when((chunk < last - HELD) | (chunk == last))
        def _():
            share_intensity(chunk)

    def halo(chunk):
        def upward():
            return pltpu.make_async_remote_copy(
                src_ref=gather_ref.at[chunk, pl.ds(own_rows, own_start)],
                dst_ref=gather_ref.at[chunk, pl.ds(0, own_start)],
                send_sem=up_sem.at[chunk],
                recv_sem=low_sem.at[chunk],
                device_id=(my_wide, my_narrow + 1),
                device_id_type=MESH,
            )

        def downward():
            return pltpu.make_async_remote_copy(
                src_ref=gather_ref.at[chunk, pl.ds(own_start, own_start)],
                dst_ref=gather_ref.at[chunk, pl.ds(own_start + own_rows, own_start)],
                send_sem=down_sem.at[chunk],
                recv_sem=high_sem.at[chunk],
                device_id=(my_wide, my_narrow - 1),
                device_id_type=MESH,
            )

        return upward, downward

    def start_halo(chunk):
        own = gather_ref.at[chunk, pl.ds(own_start, own_rows)]
        pltpu.make_async_copy(own, own, gather_sem.at[chunk]).wait()
        upward, downward = halo(chunk)

        @pl.when(my_narrow < plan.narrow - 1)
        def _():
            upward().start()

        @pl.when(my_narrow > 0)
        def _():
            downward().start()

    def build_matrix():
        extent, bins, shifts, lanes = plan.extent, plan.bins, plan.shifts, plan.lanes
        last = plan.all_bins - bins
        spread = one_hot((extent, lanes), lambda row, column: row == column // bins)
        columns = exact_dot(smooth_ref[...], spread, (0, 0))
        inner = lax.broadcasted_iota(jnp.int32, (shifts, lanes), 1) % bins
        shifted = jnp.zeros((shifts, lanes), jnp.float32)
        for offset in range(bins):
            select = one_hot(
                (shifts, extent),
                lambda row, column: column == offset - row + last + plan.half,
            )
            shifted = jnp.where(inner == offset, exact_dot(select, columns), shifted)
        shifted_ref[...] = shifted
        gather = one_hot(
            (plan.all_bins, shifts),
            lambda row, column: (column >= row)
            & (column <= row + last)
            & ((column - row) % bins == 0),
        )
        block = one_hot((lanes, lanes), lambda row, column: row // bins == column // bins)
        total = exact_dot(exact_dot(gather, shifted), block)
        mean = total * jnp.float32(1.0 / plan.all_bins)

        @pl.loop(0, chunks)
        def _(chunk):
            start = shifts - (last - bins * chunk)
            rows_here = pltpu.roll(shifted_ref[...], lax.rem(start, shifts), 0)[: plan.all_bins]
            centered = rows_here - mean
            for channel in range(BAND):
                moved = pltpu.roll(centered, bins * channel, 1) if channel else centered
                place = slice(channel * plan.all_bins, (channel + 1) * plan.all_bins)
                matrix_ref[chunk, 0, place], matrix_ref[chunk, 1, place] = split(moved)

    def smooth(chunk):
        upward, downward = halo(chunk)

        @pl.when(my_narrow > 0)
        def _():
            upward().wait_recv()

        @pl.when(my_narrow < plan.narrow - 1)
        def _():
            downward().wait_recv()

        for band in range(plan.local // BAND):
            start = band * BAND * plan.bins
            values = gather_ref[chunk, start : start + plan.reach]
            size = BAND * plan.all_bins
            place = slice(band * size, (band + 1) * size)
            total = out_ref[place]
            for side in (1, 0):
                total = total + jnp.dot(
                    matrix_ref[chunk, side, :, : plan.reach],
                    values,
                    preferred_element_type=jnp.float32,
                )
            out_ref[place] = total

    def catch_up():
        start_halo(last - 2)
        smooth(last - 3)

    @pl.loop(0, chunks + LAG)
    def _(step):
        @pl.when(step < chunks)
        def _():
            side = step % 2
            slot = step % SLOTS
            raw = raw_ref.at[side]
            pltpu.make_async_copy(raw, raw, raw_sem.at[side]).wait()

            @pl.when(step + 1 < chunks)
            def _():
                load_raw(step + 1, 1 - side)

            filter_rows(side)

            @pl.when(step >= SLOTS)
            def _():
                wait_sends(slot)

            @pl.when(step == 0)
            def _():
                pltpu.make_async_copy(table_hbm, table_ref, table_sem).wait()

            prepare()

            @pl.loop(0, plan.wide)
            def _(turn):
                block = block_at(turn)
                transform(block, slot)

                @pl.when((step == 0) & (turn == 0))
                def _():
                    pl.semaphore_wait(barrier, plan.devices - 1)

                @pl.when(step < last)
                def _():
                    start_sends(step, block, slot)

            @pl.when(step == last)
            def _():
                @pl.loop(0, plan.sets - 1)
                def _(index):
                    start_last(index, slot)

        @pl.when(step == LAG)
        def _():
            build_matrix()
            pltpu.make_async_copy(weight_ref, weight_ref, weight_sem).wait()

        @pl.when(step >= LAG)
        def _():
            form_beams(step - LAG)

        @pl.when(step == last + 1)
        def _():
            start_last(plan.sets - 1, last % SLOTS)

        @pl.when((step >= HALO_LAG) & (step <= last + 1))
        def _():
            start_halo(step - HALO_LAG)

        @pl.when((step >= SMOOTH_LAG) & (step <= last + 1))
        def _():
            smooth(step - SMOOTH_LAG)

    start_halo(last - 1)
    smooth(last - 2)
    smooth(last - 1)
    start_halo(last)
    smooth(last)

    for slot in range(min(SLOTS, chunks)):
        wait_sends(slot)

    @pl.loop(0, chunks)
    def _(chunk):
        sent = outgoing_ref.at[chunk, pl.ds(0, plan.wide - 1)]
        pltpu.make_async_copy(sent, sent, share_sem.at[chunk]).wait()
        upward, downward = halo(chunk)

        @pl.when(my_narrow < plan.narrow - 1)
        def _():
            upward().wait_send()

        @pl.when(my_narrow > 0)
        def _():
            downward().wait_send()


def fused(samples, filter_taps, table, beam_weights, smooth_kernel, plan):
    if plan.groups == 1:
        dish_split = (1, 1, plan.dishes)
    else:
        dish_split = (plan.per_pol, plan.groups, plan.rows)
    weight_shape = (plan.per_device, plan.pols, 2, *dish_split, plan.beams)
    weights = beam_weights.reshape(weight_shape)
    anywhere = pl.BlockSpec(memory_space=pl.ANY)
    local = pl.BlockSpec(memory_space=pltpu.VMEM)
    recv_shape = (plan.chunks - 1, plan.devices, plan.per_device, plan.rows, LANES)
    energy_shape = (plan.per_device * plan.bins, plan.beams)
    ext_rows = (plan.local + 2 * plan.half) * plan.bins
    out_shape = (plan.local * plan.all_bins, plan.share)
    per_chunk = pltpu.SemaphoreType.DMA((plan.chunks,))
    return pl.pallas_call(
        functools.partial(fused_kernel, plan),
        in_specs=[local, local, anywhere, anywhere, anywhere],
        out_specs=[anywhere, local],
        out_shape=[
            jax.ShapeDtypeStruct(recv_shape, jnp.bfloat16),
            pltpu.VMEM(out_shape, jnp.float32),
        ],
        scratch_shapes=[
            pltpu.VMEM(table.shape, jnp.bfloat16),
            pltpu.VMEM((2, plan.tiles, plan.inputs, 2, LANES), jnp.bfloat16),
            pltpu.VMEM((plan.halves, 2 * plan.inputs * plan.span, LANES), jnp.float32),
            pltpu.VMEM((2, plan.turns, 2 * PAIRS * plan.groups * plan.span, 2 * plan.points), jnp.bfloat16),
            pltpu.VMEM((plan.points // plan.wide * plan.rows, LANES), jnp.float32),
            pltpu.VMEM((SLOTS, plan.points, plan.rows, LANES), jnp.bfloat16),
            pltpu.VMEM(weight_shape, jnp.bfloat16),
            pltpu.VMEM((2, *recv_shape[1:]), jnp.bfloat16),
            pltpu.VMEM(energy_shape, jnp.float32),
            pltpu.VMEM((plan.shifts, plan.lanes), jnp.float32),
            pltpu.VMEM((plan.chunks, 2, BAND * plan.all_bins, plan.lanes), jnp.bfloat16),
            pltpu.VMEM(
                (plan.chunks, plan.wide, plan.per_device * plan.bins, plan.share), jnp.bfloat16
            ),
            pltpu.VMEM((plan.chunks, ext_rows, plan.share), jnp.bfloat16),
            pltpu.SemaphoreType.DMA((2,)),
            pltpu.SemaphoreType.DMA,
            pltpu.SemaphoreType.DMA,
            pltpu.SemaphoreType.DMA((SLOTS,)),
            per_chunk,
            pltpu.SemaphoreType.DMA((plan.sets,)),
            pltpu.SemaphoreType.DMA,
            *([per_chunk] * 6),
        ],
        compiler_params=pltpu.CompilerParams(
            collective_id=0, has_side_effects=True, vmem_limit_bytes=62 * 1000 * 1000
        ),
        name="fused",
    )(filter_taps, smooth_kernel, table, samples, weights)[1]


def body(samples, filter_taps, beam_weights, smooth_kernel):
    tap_count, points = filter_taps.shape
    wide_count = lax.axis_size("wide")
    narrow_count = lax.axis_size("narrow")
    per_device, pols, _, dishes, beams = beam_weights.shape
    frames = samples.shape[2] // points
    plan = Plan(
        wide=wide_count,
        narrow=narrow_count,
        inputs=samples.shape[0],
        per_device=per_device,
        points=points,
        taps=tap_count,
        pols=pols,
        dishes=dishes,
        beams=beams,
        spectra=frames - tap_count + 1,
        extent=smooth_kernel.shape[0],
    )

    def owner_of(column):
        device_slot = column // per_device
        return (
            device_slot % narrow_count * wide_count + device_slot // narrow_count
        ) * per_device + column % per_device

    table = jnp.asarray(fourier_rows(points, owner_of, wide_count))
    filtered = fused(samples, filter_taps, table, beam_weights, smooth_kernel, plan)
    return filtered.reshape(plan.local, plan.all_bins, plan.share)


def solution(mesh):
    placed = (
        P(("wide", "narrow"), None, None),
        P(),
        P(("narrow", "wide"), None, None, None, None),
        P(),
    )
    return jax.shard_map(
        body, mesh=mesh, in_specs=placed, out_specs=P("narrow", None, "wide"), check_vma=False
    )
```

```python
import dataclasses
import functools

import jax
import jax.numpy as jnp
import numpy as np
from jax import lax
from jax.experimental import pallas as pl
from jax.experimental.pallas import tpu as pltpu
from jax.sharding import PartitionSpec as P

INTEG = 8
LANES = 128
BAND = 8
SLOTS = 4
LAG = 2
PAIRS = 2
HELD = 1
HALO_LAG = 4
SMOOTH_LAG = 5
MESH = pl.DeviceIdType.MESH


@dataclasses.dataclass(frozen=True)
class Plan:
    wide: int
    narrow: int
    inputs: int
    per_device: int
    points: int
    taps: int
    pols: int
    dishes: int
    beams: int
    spectra: int
    extent: int

    @property
    def devices(self):
        return self.wide * self.narrow

    @property
    def groups(self):
        return max(1, self.inputs // 16)

    @property
    def rows(self):
        return self.inputs // self.groups

    @property
    def span(self):
        return LANES // (2 * self.groups)

    @property
    def chunks(self):
        return self.spectra // self.span

    @property
    def bins(self):
        return self.span // INTEG

    @property
    def turns(self):
        return self.rows // (2 * PAIRS)

    @property
    def together(self):
        return 8 // self.bins

    @property
    def sets(self):
        return self.per_device // self.together

    @property
    def halves(self):
        return self.points // LANES

    @property
    def tiles(self):
        return (self.span + self.taps - 1) * self.halves

    @property
    def per_pol(self):
        return self.devices // self.pols

    @property
    def half(self):
        return self.extent // 2

    @property
    def share(self):
        return self.beams // self.wide

    @property
    def local(self):
        return self.wide * self.per_device

    @property
    def all_bins(self):
        return self.spectra // INTEG

    @property
    def reach(self):
        return (BAND + self.extent - 1) * self.bins

    @property
    def lanes(self):
        return -(-self.reach // LANES) * LANES

    @property
    def shifts(self):
        return -(-(2 * self.all_bins - self.bins) // 8) * 8


def fourier_rows(points, owner_of, blocks):
    column = np.arange(points)
    phase_index = owner_of(column)[:, None] * column[None, :] % points
    angles = phase_index * (2.0 * np.pi / points)
    cosine = np.cos(angles) / np.sqrt(points)
    sine_part = np.sin(angles) / np.sqrt(points)
    real_row = np.concatenate([cosine, sine_part], axis=1)
    imag_row = np.concatenate([-sine_part, cosine], axis=1)
    table = np.stack([part.reshape(blocks, -1, 2 * points) for part in (real_row, imag_row)], axis=1)
    table = table.reshape(2 * points, 2 * points).astype(np.float32)
    high = table.astype(jnp.bfloat16)
    return np.stack([high, (table - high.astype(np.float32)).astype(jnp.bfloat16)])


def one_hot(shape, matches):
    row = lax.broadcasted_iota(jnp.int32, shape, 0)
    column = lax.broadcasted_iota(jnp.int32, shape, 1)
    return matches(row, column).astype(jnp.float32)


def exact_dot(left, right, contract=(1, 0)):
    return lax.dot_general(
        left,
        right,
        (((contract[0],), (contract[1],)), ((), ())),
        precision=lax.Precision.HIGHEST,
        preferred_element_type=jnp.float32,
    )


def split(value):
    high = value.astype(jnp.bfloat16)
    return high, (value - high.astype(jnp.float32)).astype(jnp.bfloat16)


def fused_kernel(
    plan,
    taps_ref,
    smooth_ref,
    table_hbm,
    samples_ref,
    weights_ref,
    recv_ref,
    out_ref,
    table_ref,
    raw_ref,
    window_ref,
    signal_ref,
    stage_ref,
    send_ref,
    weight_ref,
    land_ref,
    energy_ref,
    shifted_ref,
    matrix_ref,
    outgoing_ref,
    gather_ref,
    raw_sem,
    table_sem,
    weight_sem,
    send_sem,
    recv_sem,
    last_sem,
    land_sem,
    share_sem,
    gather_sem,
    up_sem,
    down_sem,
    low_sem,
    high_sem,
):
    span, rows, groups, halves = plan.span, plan.rows, plan.groups, plan.halves
    tap_count, points, chunks = plan.taps, plan.points, plan.chunks
    my_wide = lax.axis_index("wide")
    my_narrow = lax.axis_index("narrow")
    me = my_wide * plan.narrow + my_narrow

    def peer(step):
        return (
            lax.rem(my_wide + step // plan.narrow, plan.wide),
            lax.rem(my_narrow + step % plan.narrow, plan.narrow),
        )

    def load_raw(chunk, slot):
        @pl.loop(0, plan.tiles)
        def _(tile):
            column = pl.multiple_of((chunk * span * halves + tile) * LANES, LANES)
            pltpu.make_async_copy(
                samples_ref.at[:, :, pl.ds(column, LANES)], raw_ref.at[slot, tile], raw_sem.at[slot]
            ).start()

    last = chunks - 1
    own_start = plan.half * plan.bins
    own_rows = plan.local * plan.bins
    part_rows = plan.per_device * plan.bins

    barrier = pltpu.get_barrier_semaphore()
    load_raw(0, 0)
    pltpu.make_async_copy(table_hbm, table_ref, table_sem).start()

    @pl.loop(1, plan.devices)
    def _(step):
        pl.semaphore_signal(barrier, inc=1, device_id=peer(step), device_id_type=MESH)

    def set_up():
        @pl.loop(0, plan.per_device)
        def _(channel):
            pltpu.make_async_copy(
                weights_ref.at[channel], weight_ref.at[channel], weight_sem
            ).start()

        out_ref[...] = jnp.zeros_like(out_ref)

        def clear(start):
            gather_ref[:, start : start + own_start] = jnp.zeros(
                (chunks, own_start, plan.share), jnp.bfloat16
            )

        @pl.when(my_narrow == 0)
        def _():
            clear(0)

        @pl.when(my_narrow == plan.narrow - 1)
        def _():
            clear(own_start + own_rows)

    def filter_rows(slot):
        row_groups = 2 * plan.inputs // 8

        @pl.loop(0, halves * row_groups)
        def _(index):
            half = index // row_groups
            group = index % row_groups
            columns = pl.ds(pl.multiple_of(half * LANES, LANES), LANES)
            coeffs = [
                jnp.broadcast_to(taps_ref[tap : tap + 1, columns], (8, LANES))
                for tap in range(tap_count)
            ]
            sums = {}
            for frame in range(span + tap_count - 1):
                piece = raw_ref[slot, frame * halves + half, pl.ds(group * 4, 4)]
                value = piece.reshape(8, LANES).astype(jnp.float32)
                for out in range(max(0, frame - tap_count + 1), min(span - 1, frame) + 1):
                    term = coeffs[frame - out] * value
                    sums[out] = sums[out] + term if out in sums else term
                done = frame - tap_count + 1
                if done >= 0:
                    base = group * (8 * span) + done
                    window_ref[half, pl.ds(base, 8, stride=span), :] = sums.pop(done)

    def prepare():
        @pl.loop(0, plan.turns)
        def _(step):
            pieces = []
            for pair in range(PAIRS):
                for group in range(groups):
                    for member in range(2):
                        source = group * rows + step * (2 * PAIRS) + 2 * pair + member
                        blocks = []
                        for part in range(2):
                            start = pl.multiple_of((2 * source + part) * span, span)
                            for half in range(halves):
                                blocks.append(window_ref[half, pl.ds(start, span), :])
                        pieces.append(jnp.concatenate(blocks, axis=1))
            signal_ref[0, step], signal_ref[1, step] = split(jnp.concatenate(pieces, axis=0))

    def transform(block, slot):
        channels = plan.narrow * plan.per_device
        lane = lax.broadcasted_iota(jnp.int32, (channels, LANES), 1)
        first = lane % (2 * span) < span
        product = functools.partial(
            lax.dot_general,
            dimension_numbers=(((1,), (1,)), ((), ())),
            preferred_element_type=jnp.float32,
        )
        table_rows = pl.ds(pl.multiple_of(block * (2 * channels), 2 * channels), 2 * channels)

        @pl.loop(0, plan.turns)
        def _(step):
            high, low = signal_ref[0, step], signal_ref[1, step]
            result = (
                product(table_ref[1, table_rows], high)
                + product(table_ref[0, table_rows], low)
                + product(table_ref[0, table_rows], high)
            )
            for pair in range(PAIRS):
                real = result[:channels, pair * LANES : (pair + 1) * LANES]
                imag = result[channels:, pair * LANES : (pair + 1) * LANES]
                row = step * (2 * PAIRS) + 2 * pair
                stage_ref[pl.ds(row, channels, stride=rows), :] = jnp.where(
                    first, real, pltpu.roll(imag, span, 1)
                )
                stage_ref[pl.ds(row + 1, channels, stride=rows), :] = jnp.where(
                    first, pltpu.roll(real, LANES - span, 1), imag
                )

        place = pl.ds(pl.multiple_of(block * channels, channels), channels)
        send_ref[slot, place] = (
            stage_ref[...].reshape(channels, rows, LANES).astype(jnp.bfloat16)
        )

    def block_at(step):
        near = plan.wide - plan.wide // 2
        moved = jnp.where(step < plan.wide // 2, step + near, step - plan.wide // 2 + 1)
        moved = jnp.where(step == plan.wide - 1, 0, moved)
        if plan.wide & (plan.wide - 1) == 0:
            return lax.bitwise_xor(my_wide, moved)
        return lax.rem(my_wide + moved, plan.wide)

    def start_sends(chunk, block, slot):
        @pl.loop(0, plan.narrow)
        def _(step):
            if plan.narrow & (plan.narrow - 1) == 0:
                narrow = lax.bitwise_xor(my_narrow, step)
            else:
                narrow = lax.rem(my_narrow + step, plan.narrow)
            target = block * plan.narrow + narrow
            source = send_ref.at[slot, pl.ds(target * plan.per_device, plan.per_device)]

            @pl.when(target != me)
            def _():
                pltpu.make_async_remote_copy(
                    src_ref=source,
                    dst_ref=recv_ref.at[chunk, me],
                    send_sem=send_sem.at[slot],
                    recv_sem=recv_sem.at[chunk],
                    device_id=(block, narrow),
                    device_id_type=MESH,
                ).start()

            @pl.when(target == me)
            def _():
                pltpu.make_async_copy(source, recv_ref.at[chunk, me], recv_sem.at[chunk]).start()

    def start_last(index, slot):
        def voltages(target):
            first = target * plan.per_device + index * plan.together
            return send_ref.at[slot, pl.ds(first, plan.together)]

        landing = land_ref.at[1, me, pl.ds(index * plan.together, plan.together)]

        @pl.loop(1, plan.devices)
        def _(step):
            wide, narrow = peer(step)
            pltpu.make_async_remote_copy(
                src_ref=voltages(wide * plan.narrow + narrow),
                dst_ref=landing,
                send_sem=send_sem.at[slot],
                recv_sem=last_sem.at[index],
                device_id=(wide, narrow),
                device_id_type=MESH,
            ).start()

        pltpu.make_async_copy(voltages(me), landing, last_sem.at[index]).start()

    def wait_sends(slot):
        sent = send_ref.at[slot, pl.ds(0, (plan.devices - 1) * plan.per_device)]
        pltpu.make_async_copy(sent, sent, send_sem.at[slot]).wait()

    def share_intensity(chunk):
        mine = pl.ds(pl.multiple_of(own_start + my_wide * part_rows, part_rows), part_rows)

        @pl.loop(1, plan.wide)
        def _(step):
            target = lax.rem(my_wide + step, plan.wide)
            pltpu.make_async_remote_copy(
                src_ref=outgoing_ref.at[chunk, target],
                dst_ref=gather_ref.at[chunk, mine],
                send_sem=share_sem.at[chunk],
                recv_sem=gather_sem.at[chunk],
                device_id=(target, my_narrow),
                device_id_type=MESH,
            ).start()

        pltpu.make_async_copy(
            outgoing_ref.at[chunk, my_wide], gather_ref.at[chunk, mine], gather_sem.at[chunk]
        ).start()

    def form_beams(chunk):
        together = plan.together
        landed = (chunk == last).astype(jnp.int32)

        @pl.when(chunk < last)
        def _():
            arrived = recv_ref.at[chunk]
            pltpu.make_async_copy(arrived, arrived, recv_sem.at[chunk]).wait()
            landing = pltpu.make_async_copy(arrived, land_ref.at[0], land_sem)
            landing.start()
            landing.wait()

        @pl.loop(0, plan.sets)
        def _(step):
            @pl.when((chunk == last) & (step == plan.sets - 1))
            def _():
                catch_up()

            @pl.when(chunk == last)
            def _():
                arrived = land_ref.at[1, :, pl.ds(step * together, together)]
                pltpu.make_async_copy(arrived, arrived, last_sem.at[step]).wait()

            @pl.when((chunk == last) & (step == plan.sets - 1))
            def _():
                for held in range(HELD, 0, -1):
                    share_intensity(last - held)

            binned = []
            for member in range(together):
                channel = step * together + member
                energy = None
                for pol in range(plan.pols):
                    block = land_ref[landed, pol * plan.per_pol : (pol + 1) * plan.per_pol, channel]
                    block = block.astype(jnp.float32).reshape(plan.per_pol * rows, LANES)
                    turned = block.T.astype(jnp.bfloat16)
                    formed = None
                    for group in range(groups):
                        base = 2 * span * group
                        straight = turned[base : base + 2 * span]
                        crossed = jnp.concatenate(
                            [-straight[span:], straight[:span]], axis=0
                        )
                        for side, left in enumerate((straight, crossed)):
                            right = weight_ref[channel, pol, side, :, group]
                            right = right.reshape(-1, plan.beams)
                            term = jnp.dot(left, right, preferred_element_type=jnp.float32)
                            formed = term if formed is None else formed + term
                    squares = formed * formed
                    power = squares[:span] + squares[span:]
                    energy = power if energy is None else energy + power
                binned.append(energy.reshape(plan.bins, INTEG, plan.beams).sum(axis=1))
            energy_ref[pl.ds(pl.multiple_of(step * 8, 8), 8), :] = jnp.concatenate(
                binned, axis=0
            )

        scale = jnp.float32(1.0 / (plan.pols * INTEG))
        intensity = (energy_ref[...] * scale).astype(jnp.bfloat16)
        for owner in range(plan.wide):
            outgoing_ref[chunk, owner] = intensity[:, owner * plan.share : (owner + 1) * plan.share]

        @pl.when((chunk < last - HELD) | (chunk == last))
        def _():
            share_intensity(chunk)

    def halo(chunk):
        def upward():
            return pltpu.make_async_remote_copy(
                src_ref=gather_ref.at[chunk, pl.ds(own_rows, own_start)],
                dst_ref=gather_ref.at[chunk, pl.ds(0, own_start)],
                send_sem=up_sem.at[chunk],
                recv_sem=low_sem.at[chunk],
                device_id=(my_wide, my_narrow + 1),
                device_id_type=MESH,
            )

        def downward():
            return pltpu.make_async_remote_copy(
                src_ref=gather_ref.at[chunk, pl.ds(own_start, own_start)],
                dst_ref=gather_ref.at[chunk, pl.ds(own_start + own_rows, own_start)],
                send_sem=down_sem.at[chunk],
                recv_sem=high_sem.at[chunk],
                device_id=(my_wide, my_narrow - 1),
                device_id_type=MESH,
            )

        return upward, downward

    def start_halo(chunk):
        own = gather_ref.at[chunk, pl.ds(own_start, own_rows)]
        pltpu.make_async_copy(own, own, gather_sem.at[chunk]).wait()
        upward, downward = halo(chunk)

        @pl.when(my_narrow < plan.narrow - 1)
        def _():
            upward().start()

        @pl.when(my_narrow > 0)
        def _():
            downward().start()

    def build_matrix():
        extent, bins, shifts, lanes = plan.extent, plan.bins, plan.shifts, plan.lanes
        last = plan.all_bins - bins
        spread = one_hot((extent, lanes), lambda row, column: row == column // bins)
        columns = exact_dot(smooth_ref[...], spread, (0, 0))
        inner = lax.broadcasted_iota(jnp.int32, (shifts, lanes), 1) % bins
        shifted = jnp.zeros((shifts, lanes), jnp.float32)
        for offset in range(bins):
            select = one_hot(
                (shifts, extent),
                lambda row, column: column == offset - row + last + plan.half,
            )
            shifted = jnp.where(inner == offset, exact_dot(select, columns), shifted)
        shifted_ref[...] = shifted
        gather = one_hot(
            (plan.all_bins, shifts),
            lambda row, column: (column >= row)
            & (column <= row + last)
            & ((column - row) % bins == 0),
        )
        block = one_hot((lanes, lanes), lambda row, column: row // bins == column // bins)
        total = exact_dot(exact_dot(gather, shifted), block)
        mean = total * jnp.float32(1.0 / plan.all_bins)

        @pl.loop(0, chunks)
        def _(chunk):
            start = shifts - (last - bins * chunk)
            rows_here = pltpu.roll(shifted_ref[...], lax.rem(start, shifts), 0)[: plan.all_bins]
            centered = rows_here - mean
            for channel in range(BAND):
                moved = pltpu.roll(centered, bins * channel, 1) if channel else centered
                place = slice(channel * plan.all_bins, (channel + 1) * plan.all_bins)
                matrix_ref[chunk, 0, place], matrix_ref[chunk, 1, place] = split(moved)

    def smooth(chunk):
        upward, downward = halo(chunk)

        @pl.when(my_narrow > 0)
        def _():
            upward().wait_recv()

        @pl.when(my_narrow < plan.narrow - 1)
        def _():
            downward().wait_recv()

        for band in range(plan.local // BAND):
            start = band * BAND * plan.bins
            values = gather_ref[chunk, start : start + plan.reach]
            size = BAND * plan.all_bins
            place = slice(band * size, (band + 1) * size)
            total = out_ref[place]
            for side in (1, 0):
                total = total + jnp.dot(
                    matrix_ref[chunk, side, :, : plan.reach],
                    values,
                    preferred_element_type=jnp.float32,
                )
            out_ref[place] = total

    def catch_up():
        start_halo(last - 2)
        smooth(last - 3)

    @pl.loop(0, chunks + LAG)
    def _(step):
        @pl.when(step < chunks)
        def _():
            side = step % 2
            slot = step % SLOTS
            raw = raw_ref.at[side]
            pltpu.make_async_copy(raw, raw, raw_sem.at[side]).wait()

            @pl.when(step + 1 < chunks)
            def _():
                load_raw(step + 1, 1 - side)

            filter_rows(side)

            @pl.when(step >= SLOTS)
            def _():
                wait_sends(slot)

            @pl.when(step == 0)
            def _():
                pltpu.make_async_copy(table_hbm, table_ref, table_sem).wait()

            prepare()

            @pl.loop(0, plan.wide)
            def _(turn):
                block = block_at(turn)
                transform(block, slot)

                @pl.when((step == 0) & (turn == 0))
                def _():
                    pl.semaphore_wait(barrier, plan.devices - 1)

                @pl.when(step < last)
                def _():
                    start_sends(step, block, slot)

            @pl.when(step == last)
            def _():
                @pl.loop(0, plan.sets - 1)
                def _(index):
                    start_last(index, slot)

        @pl.when(step == 0)
        def _():
            set_up()

        @pl.when(step == LAG)
        def _():
            build_matrix()
            pltpu.make_async_copy(weight_ref, weight_ref, weight_sem).wait()

        @pl.when(step >= LAG)
        def _():
            form_beams(step - LAG)

        @pl.when(step == last + 1)
        def _():
            start_last(plan.sets - 1, last % SLOTS)

        @pl.when((step >= HALO_LAG) & (step <= last + 1))
        def _():
            start_halo(step - HALO_LAG)

        @pl.when((step >= SMOOTH_LAG) & (step <= last + 1))
        def _():
            smooth(step - SMOOTH_LAG)

    start_halo(last - 1)
    smooth(last - 2)
    smooth(last - 1)
    start_halo(last)
    smooth(last)

    for slot in range(min(SLOTS, chunks)):
        wait_sends(slot)

    @pl.loop(0, chunks)
    def _(chunk):
        sent = outgoing_ref.at[chunk, pl.ds(0, plan.wide - 1)]
        pltpu.make_async_copy(sent, sent, share_sem.at[chunk]).wait()
        upward, downward = halo(chunk)

        @pl.when(my_narrow < plan.narrow - 1)
        def _():
            upward().wait_send()

        @pl.when(my_narrow > 0)
        def _():
            downward().wait_send()


def fused(samples, filter_taps, table, beam_weights, smooth_kernel, plan):
    if plan.groups == 1:
        dish_split = (1, 1, plan.dishes)
    else:
        dish_split = (plan.per_pol, plan.groups, plan.rows)
    weight_shape = (plan.per_device, plan.pols, 2, *dish_split, plan.beams)
    weights = beam_weights.reshape(weight_shape)
    anywhere = pl.BlockSpec(memory_space=pl.ANY)
    local = pl.BlockSpec(memory_space=pltpu.VMEM)
    recv_shape = (plan.chunks - 1, plan.devices, plan.per_device, plan.rows, LANES)
    energy_shape = (plan.per_device * plan.bins, plan.beams)
    ext_rows = (plan.local + 2 * plan.half) * plan.bins
    out_shape = (plan.local * plan.all_bins, plan.share)
    per_chunk = pltpu.SemaphoreType.DMA((plan.chunks,))
    return pl.pallas_call(
        functools.partial(fused_kernel, plan),
        in_specs=[local, local, anywhere, anywhere, anywhere],
        out_specs=[anywhere, local],
        out_shape=[
            jax.ShapeDtypeStruct(recv_shape, jnp.bfloat16),
            pltpu.VMEM(out_shape, jnp.float32),
        ],
        scratch_shapes=[
            pltpu.VMEM(table.shape, jnp.bfloat16),
            pltpu.VMEM((2, plan.tiles, plan.inputs, 2, LANES), jnp.bfloat16),
            pltpu.VMEM((plan.halves, 2 * plan.inputs * plan.span, LANES), jnp.float32),
            pltpu.VMEM((2, plan.turns, 2 * PAIRS * plan.groups * plan.span, 2 * plan.points), jnp.bfloat16),
            pltpu.VMEM((plan.points // plan.wide * plan.rows, LANES), jnp.float32),
            pltpu.VMEM((SLOTS, plan.points, plan.rows, LANES), jnp.bfloat16),
            pltpu.VMEM(weight_shape, jnp.bfloat16),
            pltpu.VMEM((2, *recv_shape[1:]), jnp.bfloat16),
            pltpu.VMEM(energy_shape, jnp.float32),
            pltpu.VMEM((plan.shifts, plan.lanes), jnp.float32),
            pltpu.VMEM((plan.chunks, 2, BAND * plan.all_bins, plan.lanes), jnp.bfloat16),
            pltpu.VMEM(
                (plan.chunks, plan.wide, plan.per_device * plan.bins, plan.share), jnp.bfloat16
            ),
            pltpu.VMEM((plan.chunks, ext_rows, plan.share), jnp.bfloat16),
            pltpu.SemaphoreType.DMA((2,)),
            pltpu.SemaphoreType.DMA,
            pltpu.SemaphoreType.DMA,
            pltpu.SemaphoreType.DMA((SLOTS,)),
            per_chunk,
            pltpu.SemaphoreType.DMA((plan.sets,)),
            pltpu.SemaphoreType.DMA,
            *([per_chunk] * 6),
        ],
        compiler_params=pltpu.CompilerParams(
            collective_id=0, has_side_effects=True, vmem_limit_bytes=62 * 1000 * 1000
        ),
        name="fused",
    )(filter_taps, smooth_kernel, table, samples, weights)[1]


def body(samples, filter_taps, beam_weights, smooth_kernel):
    tap_count, points = filter_taps.shape
    wide_count = lax.axis_size("wide")
    narrow_count = lax.axis_size("narrow")
    per_device, pols, _, dishes, beams = beam_weights.shape
    frames = samples.shape[2] // points
    plan = Plan(
        wide=wide_count,
        narrow=narrow_count,
        inputs=samples.shape[0],
        per_device=per_device,
        points=points,
        taps=tap_count,
        pols=pols,
        dishes=dishes,
        beams=beams,
        spectra=frames - tap_count + 1,
        extent=smooth_kernel.shape[0],
    )

    def owner_of(column):
        device_slot = column // per_device
        return (
            device_slot % narrow_count * wide_count + device_slot // narrow_count
        ) * per_device + column % per_device

    table = jnp.asarray(fourier_rows(points, owner_of, wide_count))
    filtered = fused(samples, filter_taps, table, beam_weights, smooth_kernel, plan)
    return filtered.reshape(plan.local, plan.all_bins, plan.share)


def solution(mesh):
    placed = (
        P(("wide", "narrow"), None, None),
        P(),
        P(("narrow", "wide"), None, None, None, None),
        P(),
    )
    return jax.shard_map(
        body, mesh=mesh, in_specs=placed, out_specs=P("narrow", None, "wide"), check_vma=False
    )
```
